128 devices in a mesh: gx: 16 (over z_hi, x, core), gy: 8 (over z_lo, y).
Axes of the slice: x: 4, y: 4, z: 4 (z_hi: 2, z_lo: 2; z = z_hi * 2 + z_lo), core: 2. Of those that a mesh axis runs over, the one named last changes fastest.
Arguments:
- multipoles: float32 [10, 1048576], P(None, ('gx', 'gy')), may hold values from -8 to 8
- fractions: float32 [3, 1048576], P(None, ('gx', 'gy')), may hold values from 0 to 1
- base_index: int32 [3, 1048576], P(None, ('gx', 'gy')), may hold values from 0 to 252, as said below
- block_plane: int32 [8192], P(('gx', 'gy')), may hold values from 0 to 3
- atom_count: int32 [8192], P(('gx', 'gy')), may hold values from 32 to 128, as said below
- coupling: float32 [8, 256, 256], replicated, may hold values from -0.375 to 0.375
Outputs:
- coupled: float32 [2, 256, 512, 256], P(None, ('gx', 'gy'))
The draws below stay inside these ranges and needn't reach their ends.
Inputs may be any that keep to these rules, and one draw needn't show every extreme that they name: `base_index`: row 0 is an atom's x cell within its block's plane block, 0 to 7; row 1 its y cell within its device's 64 columns, 0 to 63; row 2 its z cell, 0 to 252. Atoms of the slots of device d lie in device d's cells. `atom_count`: slots of a block at or past its count are padding whose values are to be ignored.
All inputs are finite; a program needn't handle non-finite values.
Results may differ from the reference program's by a relative error of at most 0.0042.
Values sent between devices are 32-bit elements; how exact they have to be, the bound alone decides.
No kernel may reach another device: no remote copies, remote signals or barrier semaphores. Data moves between devices by JAX's collectives and lax.ppermute only.
A program may use at most 64 MiB of HBM per device.

```python
import math
import jax
import jax.numpy as jnp
from jax import lax

NX = 512
NY = 512
NZ = 256
XB = 8
SLOT_BLK = 128
MBLK = 8
KX = 256
CX = 32
CY = 64
SLOTS_DEV = 8192
BLOCKS = 8192
SLOTS = 1048576
N_GY = 8


def draw_base_index(key, part):
    keys = jax.random.split(jax.random.fold_in(key, 3), 3)
    x_part = jax.random.randint(keys[0], (SLOTS,), 0, XB)
    y_part = jax.random.randint(keys[1], (SLOTS,), 0, CY)
    z_part = jax.random.randint(keys[2], (SLOTS,), 0, NZ - 3)
    slot_ids = jnp.arange(SLOTS, dtype=jnp.int32)
    x_part = jnp.where(slot_ids == 0, XB - 1, jnp.where(slot_ids == 1, 0, x_part))
    y_part = jnp.where(slot_ids == 0, CY - 1, jnp.where(slot_ids == 1, 0, y_part))
    z_part = jnp.where(slot_ids == 0, NZ - 4, jnp.where(slot_ids == 1, 0, z_part))
    return jnp.stack([x_part, y_part, z_part]).astype(jnp.int32)


def draw_atom_count(key, part):
    counts = jax.random.randint(jax.random.fold_in(key, 5), (BLOCKS,), 32, 129)
    chosen = jax.random.randint(jax.random.fold_in(key, 6), (), 0, BLOCKS)
    block_ids = jnp.arange(BLOCKS, dtype=jnp.int32)
    return jnp.where(block_ids == chosen, 128, counts).astype(jnp.int32)


def with_ends(values, key, smallest, largest):
    longest = values.shape.index(max(values.shape))
    spots = []
    for shift in (0, 1):
        where = [jax.random.randint(jax.random.fold_in(key, axis), (), 0, length) for axis, length in enumerate(values.shape)]
        where[longest] = (where[longest] + shift) % values.shape[longest]
        spots.append(tuple(where))
    return values.at[spots[0]].set(smallest).at[spots[1]].set(largest)


def levels(rng, extent, pieces, low, high):
    def one(dim, blocks):
        draws = jax.random.uniform(jax.random.fold_in(jax.random.fold_in(rng, 6), dim), (blocks,), jnp.float32, low / len(pieces), high / len(pieces))
        return jnp.repeat(jnp.exp(draws), extent[dim] // blocks).reshape((-1,) + (1,) * (len(extent) - dim - 1))

    gain = one(*pieces[0])
    for cut in pieces[1:]:
        gain = gain * one(*cut)
    return gain


def normal_values(own_key, extent, spread, limit, cuts=(), kind=jnp.bfloat16):
    values = spread * jax.random.normal(own_key, extent, jnp.float32)
    if cuts:
        values = values * levels(own_key, extent, cuts, -0.22, 0.18)
    return jnp.clip(values, -limit, limit).astype(kind)


def setup_inputs(seed: int = 0) -> dict:
    splits = jax.random.split(jax.random.key(seed), 7)
    multipoles = normal_values(splits[0], (10, SLOTS), 2.0, 8.0, ((1, 128),), jnp.float32)
    fractions = jnp.clip(1.0 * jax.random.uniform(splits[1], (3, SLOTS), jnp.float32) ** levels(splits[1], (3, SLOTS), ((1, 128),), -0.2, 0.2), 0.0, 1.0)
    base_index = draw_base_index(jax.random.fold_in(splits[6], 71), 0)
    block_plane = with_ends(jax.random.randint(splits[3], (BLOCKS,), 0, CX // XB), jax.random.fold_in(splits[3], 1), 0, (CX // XB) - 1).astype(jnp.int32)
    atom_count = draw_atom_count(jax.random.fold_in(splits[6], 71), 0)
    coupling = normal_values(splits[5], (MBLK, NZ, NZ), NZ ** -0.5, 0.375, (), jnp.float32)
    return dict(multipoles=multipoles, fractions=fractions, base_index=base_index, block_plane=block_plane, atom_count=atom_count, coupling=coupling)


def spline_weights(fraction):
    remain = 1.0 - fraction
    square = fraction * fraction
    cubed = square * fraction
    values = jnp.stack([remain * remain * remain / 6.0, (3.0 * cubed - 6.0 * square + 4.0) / 6.0, (-3.0 * cubed + 3.0 * square + 3.0 * fraction + 1.0) / 6.0, cubed / 6.0])
    slopes = jnp.stack([-remain * remain / 2.0, (3.0 * square - 4.0 * fraction) / 2.0, (-3.0 * square + 2.0 * fraction + 1.0) / 2.0, square / 2.0])
    curves = jnp.stack([remain, 3.0 * fraction - 2.0, 1.0 - 3.0 * fraction, fraction])
    return jnp.stack([values, slopes, curves])

def plane_weights(moments, spline_x, spline_y):
    x_spline = spline_x[:, :, None]
    y_spline = spline_y[:, None, :]
    moment = moments[:, None, None]
    order_zero = moment[0] * x_spline[0] * y_spline[0] + moment[1] * x_spline[1] * y_spline[0] + moment[2] * x_spline[0] * y_spline[1] + moment[4] * x_spline[2] * y_spline[0] + moment[5] * x_spline[0] * y_spline[2] + moment[7] * x_spline[1] * y_spline[1]
    order_one = moment[3] * x_spline[0] * y_spline[0] + moment[8] * x_spline[1] * y_spline[0] + moment[9] * x_spline[0] * y_spline[1]
    order_two = moment[6] * x_spline[0] * y_spline[0]
    return jnp.stack([order_zero, order_one, order_two]).astype(jnp.bfloat16)

def reference(multipoles, fractions, base_index, block_plane, atom_count, coupling):
    slot_ids = jnp.arange(SLOTS, dtype=jnp.int32)
    block_ids = slot_ids // SLOT_BLK
    live_slot = (slot_ids % SLOT_BLK < atom_count[block_ids]).astype(jnp.float32)
    moments = multipoles * live_slot[None, :]
    device = slot_ids // SLOTS_DEV
    x_cell = device // N_GY * CX + block_plane[block_ids] * XB + base_index[0]
    y_cell = device % N_GY * CY + base_index[1]
    z_cell = base_index[2]
    planes = plane_weights(moments, spline_weights(fractions[0]), spline_weights(fractions[1]))
    planes = lax.optimization_barrier(planes).astype(jnp.float32)
    z_weights = lax.optimization_barrier(spline_weights(fractions[2]).astype(jnp.bfloat16)).astype(jnp.float32)
    contrib = jnp.einsum('kabs,kcs->abcs', planes, z_weights, precision=lax.Precision.HIGHEST)
    tap_ids = jnp.arange(4, dtype=jnp.int32)
    x_full = (x_cell[None, :] + tap_ids[:, None]) % NX
    y_full = (y_cell[None, :] + tap_ids[:, None]) % NY
    z_full = z_cell[None, :] + tap_ids[:, None]
    flat_index = (x_full[:, None, None, :] * NY + y_full[None, :, None, :]) * NZ + z_full[None, None, :, :]
    density = jnp.zeros((NX * NY * NZ,), jnp.float32).at[flat_index.reshape(-1)].add(contrib.reshape(-1))
    density = density.reshape(NX, NY, NZ)
    along_x = jnp.fft.fft(density, axis=0)[:KX]
    spectrum = jnp.fft.fft(along_x, axis=1) / math.sqrt(NX * NY)
    spectra = jnp.stack([jnp.real(spectrum), jnp.imag(spectrum)])
    blocked = spectra.reshape(2, KX, MBLK, NY // MBLK, NZ)
    coupled = jnp.einsum('ckbjw,bzw->ckbjz', blocked, coupling, precision=lax.Precision.HIGHEST)
    return coupled.reshape(2, KX, NY, NZ)
```

```python
import math

import jax
import jax.numpy as jnp
import ml_dtypes
import numpy as np
from jax import lax
from jax.experimental import pallas as pl
from jax.experimental.pallas import tpu as pltpu
from jax.sharding import PartitionSpec as P

NX = 512
NY = 512
NZ = 256
XB = 8
LANES = 128
MBLK = 8
KX = 256
TILE = 16
ROWS_Y = 80
WIN_X = XB + 3
F32 = jnp.float32
BF16 = jnp.bfloat16


def tap_constants(tap):
    def pick(c0, c1, c2, c3):
        return jnp.where(tap == 0, c0, jnp.where(tap == 1, c1, jnp.where(tap == 2, c2, c3))).astype(F32)

    return dict(
        shift=pick(1.0, 0.0, 0.0, 0.0),
        sign=pick(-1.0, 1.0, 1.0, 1.0),
        w=(pick(0.0, 2.0 / 3.0, 1.0 / 6.0, 0.0), pick(0.0, 0.0, 0.5, 0.0), pick(0.0, -1.0, 0.5, 0.0), pick(1.0 / 6.0, 0.5, -0.5, 1.0 / 6.0)),
        d=(pick(0.0, 0.0, 0.5, 0.0), pick(0.0, -2.0, 1.0, 0.0), pick(-0.5, 1.5, -1.5, 0.5)),
        s=(pick(0.0, -2.0, 1.0, 0.0), pick(1.0, 3.0, -3.0, 1.0)),
    )


def tap_values(fraction, const):
    u = const["shift"] + const["sign"] * fraction
    w0, w1, w2, w3 = const["w"]
    d0, d1, d2 = const["d"]
    s0, s1 = const["s"]
    return ((w3 * u + w2) * u + w1) * u + w0, (d2 * u + d1) * u + d0, s1 * u + s0


def spread_kernel(cells_x, cells_y, block_count, plane_ref, count_ref, moment_ref, fraction_ref, base_ref, out_ref, rim_ref,
                  raw, taps, a0, b0, a1, b1, density, stage, cursor, pair_group, pair_plane):
    planes = cells_x // XB
    spare = block_count + 2 * planes
    lane = lax.broadcasted_iota(jnp.int32, (TILE, LANES), 1)

    density[...] = jnp.zeros_like(density)

    for p in range(planes):
        cursor[p] = 0

    def tally(g, carry):
        p = plane_ref[g]
        cursor[p] = cursor[p] + count_ref[g]
        return carry

    lax.fori_loop(0, block_count, tally, 0)
    zero_group = jnp.zeros((TILE, LANES), F32)
    start = jnp.int32(0)
    pairs = jnp.int32(0)
    for p in range(planes):
        total = cursor[p]
        whole = (total + LANES - 1) // LANES
        cursor[p] = start * LANES
        raw[pl.ds(pl.multiple_of(start * TILE, TILE), TILE), :] = zero_group
        here = (whole + 1) // 2

        def note(i, carry, start=start, pairs=pairs, p=p):
            pair_group[pairs + i] = start + 2 * i
            pair_plane[pairs + i] = p
            return carry

        lax.fori_loop(0, here, note, 0)
        pairs = pairs + here
        start = start + total // LANES + 2
    for i in range(3):
        pair_group[pairs + i] = spare
        pair_plane[pairs + i] = 0
    for i in range(2):
        raw[(spare + i) * TILE:(spare + i + 1) * TILE, :] = zero_group

    def append(g, carry):
        p = plane_ref[g]
        live = count_ref[g]
        place = cursor[p]
        cursor[p] = place + live
        group = place // LANES
        offset = place % LANES
        column = pl.multiple_of(g * LANES, LANES)
        stage[0:10, :] = moment_ref[:, pl.ds(column, LANES)]
        stage[10:13, :] = fraction_ref[:, pl.ds(column, LANES)]
        stage[13:16, :] = base_ref[:, pl.ds(column, LANES)].astype(F32)
        rows = jnp.where(lane < live, stage[...], 0.0)
        rows = pltpu.roll(rows, offset, axis=1)
        first = pl.multiple_of(group * TILE, TILE)
        raw[pl.ds(first, TILE), :] = raw[pl.ds(first, TILE), :] + jnp.where(lane >= offset, rows, 0.0)
        raw[pl.ds(first + TILE, TILE), :] = jnp.where(lane < offset, rows, 0.0)
        return carry

    lax.fori_loop(0, block_count, append, 0)
    for p in range(planes):
        after = (cursor[p] + LANES - 1) // LANES
        raw[pl.ds(pl.multiple_of(after * TILE, TILE), TILE), :] = zero_group

    sub = lax.broadcasted_iota(jnp.int32, (8, LANES), 0)
    inner = tap_constants(sub % 4)
    outer = [tap_constants(sub // 4), tap_constants(2 + sub // 4)]
    tile_rows = lax.broadcasted_iota(jnp.int32, (TILE, LANES), 0).astype(F32).astype(BF16)
    none = jnp.zeros((TILE, LANES), BF16)

    def build(q, a_ref, b_ref, slot):
        for member in range(2):
            base = (pair_group[q] + member) * TILE
            first = (slot * 2 + member) * 64

            def row(r, base=base):
                return raw[pl.ds(base + r, 8, stride=0), :]

            def wide(r, base=base):
                return raw[pl.ds(base + r, TILE, stride=0), :].astype(BF16)

            def tap(r, first=first):
                return taps[pl.ds(first + r, TILE, stride=0), :].astype(BF16)

            m = [row(r) for r in range(10)]
            wx, dx, sx = tap_values(row(10), inner)
            x0 = m[0] * wx + m[1] * dx + m[4] * sx
            x1 = m[2] * wx + m[7] * dx
            x2 = m[5] * wx
            x3 = m[3] * wx + m[8] * dx
            x4 = m[9] * wx
            x5 = m[6] * wx
            for half in range(2):
                wy, dy, sy = tap_values(row(11), outer[half])
                taps[first + 8 * half:first + 8 * half + 8, :] = x0 * wy + x1 * dy + x2 * sy
                taps[first + 16 + 8 * half:first + 24 + 8 * half, :] = x3 * wy + x4 * dy
                taps[first + 32 + 8 * half:first + 40 + 8 * half, :] = x5 * wy
            wz, dz, sz = tap_values(row(12), inner)
            taps[first + 48:first + 52, :] = wz[0:4]
            taps[first + 52:first + 56, :] = dz[0:4]
            taps[first + 56:first + 60, :] = sz[0:4]

            zbase = wide(15)
            ztap = [[tap(48 + 4 * k + c) for c in range(4)] for k in range(3)]
            for t in range(NZ // TILE):
                gap = tile_rows + (TILE * t) - zbase
                hit = [gap == c for c in range(4)]
                for k in range(3):
                    value = none
                    for c in range(3, -1, -1):
                        value = jnp.where(hit[c], ztap[k][c], value)
                    b_ref[TILE * t:TILE * (t + 1), (member * 3 + k) * LANES:(member * 3 + k + 1) * LANES] = value

            ybase = wide(14)
            xbase = wide(13)
            bit2 = xbase >= 4
            xbase = xbase - jnp.where(bit2, jnp.full_like(none, 4), none)
            bit1 = xbase >= 2
            xbase = xbase - jnp.where(bit1, jnp.full_like(none, 2), none)
            bit0 = xbase >= 1
            for t in range(ROWS_Y // TILE):
                gap = tile_rows + (TILE * t) - ybase
                hit = [gap == c for c in range(4)]
                for k in range(3):
                    column = []
                    for a in range(4):
                        value = none
                        for b in range(3, -1, -1):
                            value = jnp.where(hit[b], tap(16 * k + 4 * b + a), value)
                        column.append(value)
                    for bit, step in ((bit0, 1), (bit1, 2), (bit2, 4)):
                        size = len(column)
                        column = [
                            jnp.where(bit, column[i - step] if i >= step else none, column[i] if i < size else none)
                            for i in range(size + step)
                        ]
                    for x in range(WIN_X):
                        a_ref[x * ROWS_Y + TILE * t:x * ROWS_Y + TILE * (t + 1),
                              (member * 3 + k) * LANES:(member * 3 + k + 1) * LANES] = column[x]

    def spread(q, a_ref, b_ref):
        first = pl.multiple_of(pair_plane[q] * (XB * ROWS_Y), XB * ROWS_Y)
        part = lax.dot_general(a_ref[...], b_ref[...], (((1,), (1,)), ((), ())), preferred_element_type=F32)
        for half in range(2):
            grid = density.at[half]
            grid[pl.ds(first, WIN_X * ROWS_Y), :] = (
                grid[pl.ds(first, WIN_X * ROWS_Y), :] + part[:, half * LANES:(half + 1) * LANES]
            )

    build(0, a0, b0, 0)

    def turn(i, carry):
        build(2 * i + 1, a1, b1, 1)
        spread(2 * i, a0, b0)
        build(2 * i + 2, a0, b0, 0)
        spread(2 * i + 1, a1, b1)
        return carry

    lax.fori_loop(0, (pairs + 1) // 2, turn, 0)

    lines = cells_x + 3
    width = out_ref.shape[1] // lines
    columns = width // 2
    for y in range(cells_y + 3):
        for half in range(2):
            value = density.at[half][pl.ds(y, lines, stride=ROWS_Y), :]
            if y < cells_y:
                out_ref[y // columns, pl.ds(y % columns * 2 + half, lines, stride=width), :] = value
            else:
                rim_ref[pl.ds((y - cells_y) * 2 + half, lines, stride=width), :] = value
    for r in range(6, width):
        rim_ref[pl.ds(r, lines, stride=width), :] = jnp.zeros((lines, LANES), F32)


def x_kernel(groups, cells_x, in_ref, high_ref, low_ref, out_ref, lines, narrow):
    width = 8
    for l in range(width):
        cut = slice(l * LANES, (l + 1) * LANES)
        for src in range(groups):
            lines[src * cells_x:(src + 1) * cells_x, cut] = in_ref[src, pl.ds(l, cells_x, stride=width), :]
        for src in range(groups):
            first = (src + 1) % groups * cells_x
            lines[first:first + 3, cut] = lines[first:first + 3, cut] + in_ref[src, pl.ds(cells_x * width + l, 3, stride=width), :]
    narrow[...] = lines[...].astype(BF16)
    data = narrow[...]
    result = jnp.dot(high_ref[...], data, preferred_element_type=F32) + jnp.dot(low_ref[...], data, preferred_element_type=F32)
    devices = out_ref.shape[0] // 32
    for q in range(4):
        for l in range(width):
            out_ref[pl.ds(l // 2 * 8 + q * 2 + l % 2, devices, stride=32), :] = (
                result[q * devices:(q + 1) * devices, l * LANES:(l + 1) * LANES]
            )


def y_kernel(in_ref, high_ref, low_ref, coupling_ref, out_ref, data, spectrum):
    @pl.when(pl.program_id(0) == 0)
    def _():
        for q in range(4):
            for half in range(2):
                value = in_ref[pl.ds(q * 2 + half, NY, stride=8), :]
                same = slice(q * NZ + half * LANES, q * NZ + (half + 1) * LANES)
                swap = slice((q ^ 1) * NZ + half * LANES, (q ^ 1) * NZ + (half + 1) * LANES)
                data[0:NY, same] = value.astype(BF16)
                data[NY:2 * NY, swap] = (value if q % 2 else -value).astype(BF16)
        lines = data[...]
        spectrum[...] = jnp.dot(high_ref[...], lines, preferred_element_type=F32) + jnp.dot(
            low_ref[...], lines, preferred_element_type=F32
        )

    block = NY // MBLK
    rows = spectrum[pl.ds(pl.multiple_of(pl.program_id(0) * block, block), block), :].astype(BF16)
    rows = jnp.concatenate([rows[:, q * NZ:(q + 1) * NZ] for q in range(4)], axis=0)
    weight = coupling_ref[0]
    high = weight.astype(BF16)
    low = (weight - high.astype(F32)).astype(BF16)
    dims = (((1,), (1,)), ((), ()))
    result = lax.dot_general(rows, high, dims, preferred_element_type=F32) + lax.dot_general(
        rows, low, dims, preferred_element_type=F32
    )
    for q in range(4):
        out_ref[q % 2, q // 2, :, :] = result[q * block:(q + 1) * block]


def two_parts(table):
    high = table.astype(ml_dtypes.bfloat16)
    low = (table - high.astype(np.float64)).astype(ml_dtypes.bfloat16)
    return high, low


def tables(size_x, size_y):
    devices = size_x * size_y
    wave = np.arange(KX).reshape(devices, 2).T.reshape(2, 1, devices, 1)
    angle = 2.0 * np.pi * (wave * np.arange(NX) % NX) / NX
    scale = 1.0 / math.sqrt(NX * NY)
    table_x = np.concatenate([np.cos(angle), -np.sin(angle)], 1).reshape(4 * devices, NX) * scale
    columns = NY // devices
    y = np.arange(size_y)[None, :, None] * (NY // size_y) + np.arange(size_x)[:, None, None] * columns + np.arange(columns)
    angle = 2.0 * np.pi * (np.arange(NY)[:, None] * y.reshape(1, NY) % NY) / NY
    table_y = np.concatenate([np.cos(angle), np.sin(angle)], 1)
    return two_parts(table_x), two_parts(table_y)


def per_device(multipoles, fractions, base_index, block_plane, atom_count, coupling):
    size_x = lax.axis_size("gx")
    size_y = lax.axis_size("gy")
    cells_x = NX // size_x
    cells_y = NY // size_y
    block_count = block_plane.shape[0]
    devices = size_x * size_y
    lines = cells_x + 3
    (x_high, x_low), (y_high, y_low) = tables(size_x, size_y)
    groups = block_count + 2 * (cells_x // XB) + 2
    vmem = pltpu.VMEM
    smem = pl.BlockSpec(memory_space=pltpu.SMEM)
    whole = pl.BlockSpec(memory_space=pltpu.VMEM)
    limit = pltpu.CompilerParams(vmem_limit_bytes=56 << 20)

    density, rim = pl.pallas_call(
        lambda *refs: spread_kernel(cells_x, cells_y, block_count, *refs),
        out_shape=(
            jax.ShapeDtypeStruct((size_x, lines * 8, LANES), F32),
            jax.ShapeDtypeStruct((lines * 8, LANES), F32),
        ),
        in_specs=[smem, smem, whole, whole, whole],
        out_specs=(whole, whole),
        scratch_shapes=[
            vmem((groups * TILE, LANES), F32),
            vmem((256, LANES), F32),
            vmem((WIN_X * ROWS_Y, 6 * LANES), BF16),
            vmem((NZ, 6 * LANES), BF16),
            vmem((WIN_X * ROWS_Y, 6 * LANES), BF16),
            vmem((NZ, 6 * LANES), BF16),
            vmem((2, lines * ROWS_Y, LANES), F32),
            vmem((TILE, LANES), F32),
            pltpu.SMEM((8,), jnp.int32),
            pltpu.SMEM((block_count + 16,), jnp.int32),
            pltpu.SMEM((block_count + 16,), jnp.int32),
        ],
        compiler_params=limit,
        name="spread",
    )(block_plane, atom_count, multipoles, fractions, base_index)

    rim = lax.ppermute(rim, "gy", [(i, (i + 1) % size_y) for i in range(size_y)])
    density = density.at[0].add(rim)
    density = lax.all_to_all(density, "gx", split_axis=0, concat_axis=0, tiled=True)

    spectrum = pl.pallas_call(
        lambda *refs: x_kernel(size_x, cells_x, *refs),
        out_shape=jax.ShapeDtypeStruct((devices * 32, LANES), F32),
        in_specs=[whole] * 3,
        out_specs=whole,
        scratch_shapes=[vmem((NX, 8 * LANES), F32), vmem((NX, 8 * LANES), BF16)],
        compiler_params=limit,
        name="transform_x",
    )(density, jnp.asarray(x_high), jnp.asarray(x_low))

    spectrum = lax.all_to_all(
        spectrum.reshape(devices, 32, LANES), ("gx", "gy"), split_axis=0, concat_axis=0, tiled=True
    ).reshape(devices * 32, LANES)

    fixed = lambda i: (0, 0)
    return pl.pallas_call(
        y_kernel,
        out_shape=jax.ShapeDtypeStruct((2, 2, NY, NZ), F32),
        grid=(MBLK,),
        in_specs=[
            pl.BlockSpec((devices * 32, LANES), fixed, pipeline_mode=pl.Buffered(1)),
            pl.BlockSpec((NY, 2 * NY), fixed, pipeline_mode=pl.Buffered(1)),
            pl.BlockSpec((NY, 2 * NY), fixed, pipeline_mode=pl.Buffered(1)),
            pl.BlockSpec((1, NZ, NZ), lambda i: (i, 0, 0)),
        ],
        out_specs=pl.BlockSpec((2, 2, NY // MBLK, NZ), lambda i: (0, 0, i, 0)),
        scratch_shapes=[vmem((2 * NY, 4 * NZ), BF16), vmem((NY, 4 * NZ), F32)],
        compiler_params=limit,
        name="transform_y",
    )(spectrum, jnp.asarray(y_high), jnp.asarray(y_low), coupling)


def solution(mesh):
    return jax.shard_map(
        per_device,
        mesh=mesh,
        in_specs=(
            P(None, ("gx", "gy")),
            P(None, ("gx", "gy")),
            P(None, ("gx", "gy")),
            P(("gx", "gy")),
            P(("gx", "gy")),
            P(),
        ),
        out_specs=P(None, ("gx", "gy"), None, None),
        check_vma=False,
    )
```

```python
import math

import jax
import jax.numpy as jnp
import ml_dtypes
import numpy as np
from jax import lax
from jax.experimental import pallas as pl
from jax.experimental.pallas import tpu as pltpu
from jax.sharding import PartitionSpec as P

NX = 512
NY = 512
NZ = 256
XB = 8
LANES = 128
MBLK = 8
KX = 256
TILE = 16
ROWS_Y = 64
WIN_X = XB + 3
ROWS = WIN_X * ROWS_Y + 3 * TILE
BATCH = 8
BUILD_STEPS = 3
CHUNKS = ((0, 128), (128, 128), (256, 128), (384, 128), (512, 128), (640, 112))
F32 = jnp.float32
BF16 = jnp.bfloat16


def tap_constants(tap):
    def pick(c0, c1, c2, c3):
        return jnp.where(tap == 0, c0, jnp.where(tap == 1, c1, jnp.where(tap == 2, c2, c3))).astype(F32)

    return dict(
        shift=pick(1.0, 0.0, 0.0, 0.0),
        sign=pick(-1.0, 1.0, 1.0, 1.0),
        w=(pick(0.0, 2.0 / 3.0, 1.0 / 6.0, 0.0), pick(0.0, 0.0, 0.5, 0.0), pick(0.0, -1.0, 0.5, 0.0), pick(1.0 / 6.0, 0.5, -0.5, 1.0 / 6.0)),
        d=(pick(0.0, 0.0, 0.5, 0.0), pick(0.0, -2.0, 1.0, 0.0), pick(-0.5, 1.5, -1.5, 0.5)),
        s=(pick(0.0, -2.0, 1.0, 0.0), pick(1.0, 3.0, -3.0, 1.0)),
    )


def tap_values(fraction, const):
    u = const["shift"] + const["sign"] * fraction
    w0, w1, w2, w3 = const["w"]
    d0, d1, d2 = const["d"]
    s0, s1 = const["s"]
    return ((w3 * u + w2) * u + w1) * u + w0, (d2 * u + d1) * u + d0, s1 * u + s0


def spread_kernel(cells_x, cells_y, block_count, plane_in, count_in, moment_in, fraction_in, base_in, out_ref, rim_ref,
                  plane_ref, count_ref, moment_ref, fraction_ref, base_ref, arrived, raw, taps, a0, b0, a1, b1, density, edge, stage, cursor, pair_group, pair_plane, pair_last):
    planes = cells_x // XB
    spare = block_count + 2 * planes
    lane = lax.broadcasted_iota(jnp.int32, (TILE, LANES), 1)

    copies = [
        pltpu.make_async_copy(source, target, arrived.at[i])
        for i, (source, target) in enumerate(
            (
                (plane_in, plane_ref),
                (count_in, count_ref),
                (moment_in, moment_ref),
                (fraction_in, fraction_ref),
                (base_in, base_ref),
            )
        )
    ]
    for copy in copies:
        copy.start()
    density[...] = jnp.zeros_like(density)
    edge[...] = jnp.zeros_like(edge)

    copies[0].wait()
    copies[1].wait()

    for p in range(planes):
        cursor[p] = 0

    def tally(g, carry):
        p = plane_ref[g]
        cursor[p] = cursor[p] + count_ref[g]
        return carry

    lax.fori_loop(0, block_count, tally, 0)
    zero_group = jnp.zeros((TILE, LANES), F32)
    start = jnp.int32(0)
    pairs = jnp.int32(0)
    for p in range(planes):
        total = cursor[p]
        whole = (total + LANES - 1) // LANES
        cursor[p] = start * LANES
        raw[pl.ds(pl.multiple_of(start * TILE, TILE), TILE), :] = zero_group
        here = (whole + 1) // 2

        def note(i, carry, start=start, pairs=pairs, here=here, p=p):
            pair_group[pairs + i] = start + 2 * i
            pair_plane[pairs + i] = p
            pair_last[pairs + i] = jnp.where(i == here - 1, 1, 0)
            return carry

        lax.fori_loop(0, here, note, 0)
        pairs = pairs + here
        start = start + total // LANES + 2
    for i in range(3):
        pair_group[pairs + i] = spare
        pair_plane[pairs + i] = 0
        pair_last[pairs + i] = 1
    for i in range(2):
        raw[(spare + i) * TILE:(spare + i + 1) * TILE, :] = zero_group

    for copy in copies[2:]:
        copy.wait()

    def append(i, carry):
        moved = []
        for k in range(BATCH):
            g = i * BATCH + k
            column = pl.multiple_of(g * LANES, LANES)
            stage[k, 0:10, :] = moment_ref[:, pl.ds(column, LANES)]
            stage[k, 10:13, :] = fraction_ref[:, pl.ds(column, LANES)]
            stage[k, 13:16, :] = base_ref[:, pl.ds(column, LANES)].astype(F32)
        for k in range(BATCH):
            g = i * BATCH + k
            p = plane_ref[g]
            live = count_ref[g]
            place = cursor[p]
            cursor[p] = place + live
            offset = place % LANES
            rows = pltpu.roll(jnp.where(lane < live, stage[k], 0.0), offset, axis=1)
            moved.append((pl.multiple_of(place // LANES * TILE, TILE), lane >= offset, rows))
        for first, keep, rows in moved:
            raw[pl.ds(first, TILE), :] = raw[pl.ds(first, TILE), :] + jnp.where(keep, rows, 0.0)
            raw[pl.ds(first + TILE, TILE), :] = jnp.where(keep, 0.0, rows)
        return carry

    lax.fori_loop(0, block_count // BATCH, append, 0)
    for p in range(planes):
        after = (cursor[p] + LANES - 1) // LANES
        raw[pl.ds(pl.multiple_of(after * TILE, TILE), TILE), :] = zero_group

    sub = lax.broadcasted_iota(jnp.int32, (8, LANES), 0)
    inner = tap_constants(sub % 4)
    outer = [tap_constants(sub // 4), tap_constants(2 + sub // 4)]
    tile_rows = lax.broadcasted_iota(jnp.int32, (TILE, LANES), 0).astype(F32).astype(BF16)
    none = jnp.zeros((TILE, LANES), BF16)
    tile_iota = lax.broadcasted_iota(jnp.int32, (TILE, LANES), 0)
    edge_x = (tile_iota // 4).astype(F32).astype(BF16)
    edge_y = (cells_y + tile_iota % 4).astype(F32).astype(BF16)

    def build(q, a_ref, b_ref, slot):
        for member in range(2):
            base = (pair_group[q] + member) * TILE
            first = (slot * 2 + member) * 64

            def row(r, base=base):
                return raw[pl.ds(base + r, 8, stride=0), :]

            def wide(r, base=base):
                return raw[pl.ds(base + r, TILE, stride=0), :].astype(BF16)

            def tap(r, first=first):
                return taps[pl.ds(first + r, TILE, stride=0), :].astype(BF16)

            m = [row(r) for r in range(10)]
            wx, dx, sx = tap_values(row(10), inner)
            x0 = m[0] * wx + m[1] * dx + m[4] * sx
            x1 = m[2] * wx + m[7] * dx
            x2 = m[5] * wx
            x3 = m[3] * wx + m[8] * dx
            x4 = m[9] * wx
            x5 = m[6] * wx
            for half in range(2):
                wy, dy, sy = tap_values(row(11), outer[half])
                taps[first + 8 * half:first + 8 * half + 8, :] = x0 * wy + x1 * dy + x2 * sy
                taps[first + 16 + 8 * half:first + 24 + 8 * half, :] = x3 * wy + x4 * dy
                taps[first + 32 + 8 * half:first + 40 + 8 * half, :] = x5 * wy
            wz, dz, sz = tap_values(row(12), inner)
            taps[first + 48:first + 52, :] = wz[0:4]
            taps[first + 52:first + 56, :] = dz[0:4]
            taps[first + 56:first + 60, :] = sz[0:4]

            zbase = wide(15)
            ztap = [[tap(48 + 4 * k + c) for c in range(4)] for k in range(3)]
            for t in range(NZ // TILE):
                gap = tile_rows + (TILE * t) - zbase
                hit = [gap == c for c in range(4)]
                for k in range(3):
                    value = none
                    for c in range(3, -1, -1):
                        value = jnp.where(hit[c], ztap[k][c], value)
                    b_ref[TILE * t:TILE * (t + 1), (member * 3 + k) * LANES:(member * 3 + k + 1) * LANES] = value
                yield

            ybase = wide(14)
            xbase = wide(13)
            gap = edge_y - ybase
            hit = [gap == c for c in range(4)]
            where_x = [[edge_x + 4 * m - xbase == c for c in range(4)] for m in range(3)]
            for k in range(3):
                column = []
                for a in range(4):
                    value = none
                    for b in range(3, -1, -1):
                        value = jnp.where(hit[b], tap(16 * k + 4 * b + a), value)
                    column.append(value)
                for m in range(3):
                    value = none
                    for a in range(3, -1, -1):
                        value = jnp.where(where_x[m][a], column[a], value)
                    a_ref[WIN_X * ROWS_Y + TILE * m:WIN_X * ROWS_Y + TILE * (m + 1),
                          (member * 3 + k) * LANES:(member * 3 + k + 1) * LANES] = value
                yield
            bit2 = xbase >= 4
            xbase = xbase - jnp.where(bit2, jnp.full_like(none, 4), none)
            bit1 = xbase >= 2
            xbase = xbase - jnp.where(bit1, jnp.full_like(none, 2), none)
            bit0 = xbase >= 1
            for t in range(ROWS_Y // TILE):
                gap = tile_rows + (TILE * t) - ybase
                hit = [gap == c for c in range(4)]
                for k in range(3):
                    column = []
                    for a in range(4):
                        value = none
                        for b in range(3, -1, -1):
                            value = jnp.where(hit[b], tap(16 * k + 4 * b + a), value)
                        column.append(value)
                    for bit, step in ((bit0, 1), (bit1, 2), (bit2, 4)):
                        size = len(column)
                        column = [
                            jnp.where(bit, column[i - step] if i >= step else none, column[i] if i < size else none)
                            for i in range(size + step)
                        ]
                    for x in range(WIN_X):
                        a_ref[x * ROWS_Y + TILE * t:x * ROWS_Y + TILE * (t + 1),
                              (member * 3 + k) * LANES:(member * 3 + k + 1) * LANES] = column[x]
                    yield

    def multiply(sums, a_ref, b_ref):
        def push(part, unit, register):
            cut = slice(part * 2 * LANES, (part + 1) * 2 * LANES)
            pltpu.matmul_push_rhs(b_ref[:, cut], register, unit, transpose=True)

        def add(part, unit, i, register):
            row, size = CHUNKS[i]
            lhs = a_ref[row:row + size, part * 2 * LANES:(part + 1) * 2 * LANES]
            pltpu.matmul_acc_lhs(sums[unit * len(CHUNKS) + i], lhs, load_staged_rhs=register)

        push(0, 0, 0)
        push(1, 1, 0)
        yield
        for i in range(len(CHUNKS)):
            for unit in range(2):
                add(unit, unit, i, None if i else 0)
                yield
            if i < 2:
                push(2, i, 1)
        for i in range(len(CHUNKS) // 2):
            for unit in range(2):
                add(2, unit, i + unit * (len(CHUNKS) // 2), None if i else 1)
                yield

    def flush(sums, plane):
        main = WIN_X * ROWS_Y
        first = pl.multiple_of(plane * (XB * ROWS_Y), XB * ROWS_Y)
        corner = pl.multiple_of(plane * (XB * 4), XB * 4)
        for i, (row, size) in enumerate(CHUNKS):
            part = pltpu.matmul_pop(sums[i]) + pltpu.matmul_pop(sums[len(CHUNKS) + i])
            inside = min(size, main - row)
            for half in range(2):
                cut = slice(half * LANES, (half + 1) * LANES)
                grid, rim = density.at[half], edge.at[half]
                grid[pl.ds(first + row, inside), :] = grid[pl.ds(first + row, inside), :] + part[:inside, cut]
                if inside < size:
                    rim[pl.ds(corner, size - inside), :] = rim[pl.ds(corner, size - inside), :] + part[inside:, cut]

    def step(sums, q, now, later, slot):
        steps = multiply(sums, *now)
        for i, _ in enumerate(build(q + 1, *later, slot)):
            if i % BUILD_STEPS == 0:
                next(steps, None)
        for _ in steps:
            pass

        @pl.when(pair_last[q] == 1)
        def _():
            flush(sums, pair_plane[q])

    for _ in build(0, a0, b0, 0):
        pass

    def turns(*sums):
        def turn(i, carry):
            step(sums, 2 * i, (a0, b0), (a1, b1), 1)
            step(sums, 2 * i + 1, (a1, b1), (a0, b0), 0)
            return carry

        lax.fori_loop(0, (pairs + 1) // 2, turn, 0)

    pl.run_scoped(turns, *[pltpu.ACC(unit)((size, NZ), F32) for unit in range(2) for _, size in CHUNKS])

    lines = cells_x + 3
    width = out_ref.shape[1] // lines
    columns = width // 2
    for half in range(2):
        for y in range(cells_y):
            out_ref[y // columns, pl.ds(y % columns * 2 + half, lines, stride=width), :] = (
                density.at[half][pl.ds(y, lines, stride=ROWS_Y), :]
            )
        for y in range(3):
            rim_ref[pl.ds(y * 2 + half, lines, stride=width), :] = edge.at[half][pl.ds(y, lines, stride=4), :]
    for r in range(6, width):
        rim_ref[pl.ds(r, lines, stride=width), :] = jnp.zeros((lines, LANES), F32)


def x_kernel(groups, cells_x, in_ref, high_ref, low_ref, out_ref, lines, narrow):
    width = 8
    for l in range(width):
        cut = slice(l * LANES, (l + 1) * LANES)
        for src in range(groups):
            lines[src * cells_x:(src + 1) * cells_x, cut] = in_ref[src, pl.ds(l, cells_x, stride=width), :]
        for src in range(groups):
            first = (src + 1) % groups * cells_x
            lines[first:first + 3, cut] = lines[first:first + 3, cut] + in_ref[src, pl.ds(cells_x * width + l, 3, stride=width), :]
    narrow[...] = lines[...].astype(BF16)
    data = narrow[...]
    result = jnp.dot(high_ref[...], data, preferred_element_type=F32) + jnp.dot(low_ref[...], data, preferred_element_type=F32)
    devices = out_ref.shape[0] // 32
    for q in range(4):
        for l in range(width):
            out_ref[pl.ds(l // 2 * 8 + q * 2 + l % 2, devices, stride=32), :] = (
                result[q * devices:(q + 1) * devices, l * LANES:(l + 1) * LANES]
            )


def y_kernel(in_ref, high_ref, low_ref, coupling_ref, out_ref, data, spectrum):
    @pl.when(pl.program_id(0) == 0)
    def _():
        half_y = NY // 2
        sums = []
        for odd in range(2):
            for q in range(4):
                for half in range(2):
                    value = in_ref[pl.ds(odd * 8 + q * 2 + half, half_y, stride=16), :]
                    same = slice(q * NZ + half * LANES, q * NZ + (half + 1) * LANES)
                    swap = slice((q ^ 1) * NZ + half * LANES, (q ^ 1) * NZ + (half + 1) * LANES)
                    data[odd, 0:half_y, same] = value.astype(BF16)
                    data[odd, half_y:NY, swap] = (value if q % 2 else -value).astype(BF16)
            lines = data[odd]
            sums.append(
                jnp.dot(high_ref[odd], lines, preferred_element_type=F32)
                + jnp.dot(low_ref[odd], lines, preferred_element_type=F32)
            )
        even, odd = sums
        spectrum[0:half_y, :] = (even + odd).astype(BF16)
        spectrum[half_y:NY, :] = (even - odd).astype(BF16)

    block = NY // MBLK
    rows = spectrum[pl.ds(pl.multiple_of(pl.program_id(0) * block, block), block), :]
    rows = jnp.concatenate([rows[:, q * NZ:(q + 1) * NZ] for q in range(4)], axis=0)
    weight = coupling_ref[0]
    high = weight.astype(BF16)
    low = (weight - high.astype(F32)).astype(BF16)
    dims = (((1,), (1,)), ((), ()))
    result = lax.dot_general(rows, high, dims, preferred_element_type=F32) + lax.dot_general(
        rows, low, dims, preferred_element_type=F32
    )
    for q in range(4):
        out_ref[q % 2, q // 2, :, :] = result[q * block:(q + 1) * block]


def two_parts(table):
    high = table.astype(ml_dtypes.bfloat16)
    low = (table - high.astype(np.float64)).astype(ml_dtypes.bfloat16)
    return high, low


def tables(size_x, size_y):
    devices = size_x * size_y
    wave = np.arange(KX).reshape(devices, 2).T.reshape(2, 1, devices, 1)
    angle = 2.0 * np.pi * (wave * np.arange(NX) % NX) / NX
    scale = 1.0 / math.sqrt(NX * NY)
    table_x = np.concatenate([np.cos(angle), -np.sin(angle)], 1).reshape(4 * devices, NX) * scale
    columns = NY // devices
    y = np.arange(size_y)[None, :, None] * (NY // size_y) + np.arange(size_x)[:, None, None] * columns + np.arange(columns)
    y = y.reshape(NY // 2, 2).T.reshape(2, 1, NY // 2)
    angle = 2.0 * np.pi * (np.arange(NY // 2)[None, :, None] * y % NY) / NY
    table_y = np.concatenate([np.cos(angle), np.sin(angle)], 2)
    return two_parts(table_x), two_parts(table_y)


def make_spread(block_count, cells_x, cells_y, size_x):
    lines = cells_x + 3
    groups = block_count + 2 * (cells_x // XB) + 2
    vmem = pltpu.VMEM
    slots = block_count * LANES
    whole = pl.BlockSpec(memory_space=pltpu.VMEM)
    return pl.pallas_call(
        lambda *refs: spread_kernel(cells_x, cells_y, block_count, *refs),
        out_shape=(
            jax.ShapeDtypeStruct((size_x, lines * 8, LANES), F32),
            jax.ShapeDtypeStruct((lines * 8, LANES), F32),
        ),
        in_specs=[pl.BlockSpec(memory_space=pltpu.MemorySpace.HBM)] * 5,
        out_specs=(whole, whole),
        scratch_shapes=[
            pltpu.SMEM((block_count,), jnp.int32),
            pltpu.SMEM((block_count,), jnp.int32),
            vmem((10, slots), F32),
            vmem((3, slots), F32),
            vmem((3, slots), jnp.int32),
            pltpu.SemaphoreType.DMA((5,)),
            vmem((groups * TILE, LANES), F32),
            vmem((256, LANES), F32),
            vmem((ROWS, 6 * LANES), BF16),
            vmem((NZ, 6 * LANES), BF16),
            vmem((ROWS, 6 * LANES), BF16),
            vmem((NZ, 6 * LANES), BF16),
            vmem((2, lines * ROWS_Y, LANES), F32),
            vmem((2, (lines + 1) * 4, LANES), F32),
            vmem((BATCH, TILE, LANES), F32),
            pltpu.SMEM((8,), jnp.int32),
            pltpu.SMEM((block_count + 16,), jnp.int32),
            pltpu.SMEM((block_count + 16,), jnp.int32),
            pltpu.SMEM((block_count + 16,), jnp.int32),
        ],
        compiler_params=pltpu.CompilerParams(vmem_limit_bytes=20 << 20),
        name="spread",
    )


def per_device(multipoles, fractions, base_index, block_plane, atom_count, coupling):
    size_x = lax.axis_size("gx")
    size_y = lax.axis_size("gy")
    cells_x = NX // size_x
    cells_y = NY // size_y
    block_count = block_plane.shape[0]
    devices = size_x * size_y
    (x_high, x_low), (y_high, y_low) = tables(size_x, size_y)
    vmem = pltpu.VMEM
    whole = pl.BlockSpec(memory_space=pltpu.VMEM)
    limit = pltpu.CompilerParams(vmem_limit_bytes=20 << 20)

    hbm = pltpu.MemorySpace.HBM
    atoms = (block_plane, atom_count, multipoles, fractions, base_index)
    density, rim = make_spread(block_count, cells_x, cells_y, size_x)(
        *[pltpu.with_memory_space_constraint(array, hbm) for array in atoms]
    )

    rim = lax.ppermute(rim, "gy", [(i, (i + 1) % size_y) for i in range(size_y)])
    density = density.at[0].add(rim)
    density = lax.all_to_all(density, "gx", split_axis=0, concat_axis=0, tiled=True)

    spectrum = pl.pallas_call(
        lambda *refs: x_kernel(size_x, cells_x, *refs),
        out_shape=jax.ShapeDtypeStruct((devices * 32, LANES), F32),
        in_specs=[whole] * 3,
        out_specs=whole,
        scratch_shapes=[vmem((NX, 8 * LANES), F32), vmem((NX, 8 * LANES), BF16)],
        compiler_params=limit,
        name="transform_x",
    )(density, jnp.asarray(x_high), jnp.asarray(x_low))

    spectrum = lax.all_to_all(
        spectrum.reshape(devices, 32, LANES), ("gx", "gy"), split_axis=0, concat_axis=0, tiled=True
    ).reshape(devices * 32, LANES)

    fixed = lambda i: (0, 0)
    return pl.pallas_call(
        y_kernel,
        out_shape=jax.ShapeDtypeStruct((2, 2, NY, NZ), F32),
        grid=(MBLK,),
        in_specs=[
            pl.BlockSpec((devices * 32, LANES), fixed, pipeline_mode=pl.Buffered(1)),
            pl.BlockSpec((2, NY // 2, NY), lambda i: (0, 0, 0), pipeline_mode=pl.Buffered(1)),
            pl.BlockSpec((2, NY // 2, NY), lambda i: (0, 0, 0), pipeline_mode=pl.Buffered(1)),
            pl.BlockSpec((1, NZ, NZ), lambda i: (i, 0, 0)),
        ],
        out_specs=pl.BlockSpec((2, 2, NY // MBLK, NZ), lambda i: (0, 0, i, 0)),
        scratch_shapes=[vmem((2, NY, 4 * NZ), BF16), vmem((NY, 4 * NZ), BF16)],
        compiler_params=limit,
        name="transform_y",
    )(spectrum, jnp.asarray(y_high), jnp.asarray(y_low), coupling)


def solution(mesh):
    return jax.shard_map(
        per_device,
        mesh=mesh,
        in_specs=(
            P(None, ("gx", "gy")),
            P(None, ("gx", "gy")),
            P(None, ("gx", "gy")),
            P(("gx", "gy")),
            P(("gx", "gy")),
            P(),
        ),
        out_specs=P(None, ("gx", "gy"), None, None),
        check_vma=False,
    )
```

```python
import math

import jax
import jax.numpy as jnp
import ml_dtypes
import numpy as np
from jax import lax
from jax.experimental import pallas as pl
from jax.experimental.pallas import tpu as pltpu
from jax.sharding import PartitionSpec as P

NX = 512
NY = 512
NZ = 256
XB = 8
LANES = 128
MBLK = 8
KX = 256
TILE = 16
ROWS_Y = 64
WIN_X = XB + 3
ROWS = WIN_X * ROWS_Y + 3 * TILE
BATCH = 8
BUILD_STEPS = 3
CHUNKS = ((0, 128), (128, 128), (256, 128), (384, 128), (512, 128), (640, 112))
F32 = jnp.float32
BF16 = jnp.bfloat16


def tap_constants(tap):
    def pick(c0, c1, c2, c3):
        return jnp.where(tap == 0, c0, jnp.where(tap == 1, c1, jnp.where(tap == 2, c2, c3))).astype(F32)

    return dict(
        shift=pick(1.0, 0.0, 0.0, 0.0),
        sign=pick(-1.0, 1.0, 1.0, 1.0),
        w=(pick(0.0, 2.0 / 3.0, 1.0 / 6.0, 0.0), pick(0.0, 0.0, 0.5, 0.0), pick(0.0, -1.0, 0.5, 0.0), pick(1.0 / 6.0, 0.5, -0.5, 1.0 / 6.0)),
        d=(pick(0.0, 0.0, 0.5, 0.0), pick(0.0, -2.0, 1.0, 0.0), pick(-0.5, 1.5, -1.5, 0.5)),
        s=(pick(0.0, -2.0, 1.0, 0.0), pick(1.0, 3.0, -3.0, 1.0)),
    )


def tap_values(fraction, const):
    u = const["shift"] + const["sign"] * fraction
    w0, w1, w2, w3 = const["w"]
    d0, d1, d2 = const["d"]
    s0, s1 = const["s"]
    return ((w3 * u + w2) * u + w1) * u + w0, (d2 * u + d1) * u + d0, s1 * u + s0


def spread_kernel(cells_x, cells_y, block_count, plane_in, count_in, moment_in, fraction_in, base_in, density, rim_ref,
                  plane_ref, count_ref, moment_ref, fraction_ref, base_ref, arrived, raw, taps, a0, b0, a1, b1, edge, stage, cursor, pair_group, pair_plane, pair_last):
    planes = cells_x // XB
    spare = block_count + 2 * planes
    lane = lax.broadcasted_iota(jnp.int32, (TILE, LANES), 1)

    copies = [
        pltpu.make_async_copy(source, target, arrived.at[i])
        for i, (source, target) in enumerate(
            (
                (plane_in, plane_ref),
                (count_in, count_ref),
                (moment_in, moment_ref),
                (fraction_in, fraction_ref),
                (base_in, base_ref),
            )
        )
    ]
    for copy in copies:
        copy.start()
    density[...] = jnp.zeros_like(density)
    edge[...] = jnp.zeros_like(edge)

    copies[0].wait()
    copies[1].wait()

    for p in range(planes):
        cursor[p] = 0

    def tally(g, carry):
        p = plane_ref[g]
        cursor[p] = cursor[p] + count_ref[g]
        return carry

    lax.fori_loop(0, block_count, tally, 0)
    zero_group = jnp.zeros((TILE, LANES), F32)
    start = jnp.int32(0)
    pairs = jnp.int32(0)
    for p in range(planes):
        total = cursor[p]
        whole = (total + LANES - 1) // LANES
        cursor[p] = start * LANES
        raw[pl.ds(pl.multiple_of(start * TILE, TILE), TILE), :] = zero_group
        here = (whole + 1) // 2

        def note(i, carry, start=start, pairs=pairs, here=here, p=p):
            pair_group[pairs + i] = start + 2 * i
            pair_plane[pairs + i] = p
            pair_last[pairs + i] = jnp.where(i == here - 1, 1, 0)
            return carry

        lax.fori_loop(0, here, note, 0)
        pairs = pairs + here
        start = start + total // LANES + 2
    for i in range(3):
        pair_group[pairs + i] = spare
        pair_plane[pairs + i] = 0
        pair_last[pairs + i] = 1
    for i in range(2):
        raw[(spare + i) * TILE:(spare + i + 1) * TILE, :] = zero_group

    for copy in copies[2:]:
        copy.wait()

    def append(i, carry):
        moved = []
        for k in range(BATCH):
            g = i * BATCH + k
            column = pl.multiple_of(g * LANES, LANES)
            stage[k, 0:10, :] = moment_ref[:, pl.ds(column, LANES)]
            stage[k, 10:13, :] = fraction_ref[:, pl.ds(column, LANES)]
            stage[k, 13:16, :] = base_ref[:, pl.ds(column, LANES)].astype(F32)
        for k in range(BATCH):
            g = i * BATCH + k
            p = plane_ref[g]
            live = count_ref[g]
            place = cursor[p]
            cursor[p] = place + live
            offset = place % LANES
            rows = pltpu.roll(jnp.where(lane < live, stage[k], 0.0), offset, axis=1)
            moved.append((pl.multiple_of(place // LANES * TILE, TILE), lane >= offset, rows))
        for first, keep, rows in moved:
            raw[pl.ds(first, TILE), :] = raw[pl.ds(first, TILE), :] + jnp.where(keep, rows, 0.0)
            raw[pl.ds(first + TILE, TILE), :] = jnp.where(keep, 0.0, rows)
        return carry

    lax.fori_loop(0, block_count // BATCH, append, 0)
    for p in range(planes):
        after = (cursor[p] + LANES - 1) // LANES
        raw[pl.ds(pl.multiple_of(after * TILE, TILE), TILE), :] = zero_group

    sub = lax.broadcasted_iota(jnp.int32, (8, LANES), 0)
    inner = tap_constants(sub % 4)
    outer = [tap_constants(sub // 4), tap_constants(2 + sub // 4)]
    tile_rows = lax.broadcasted_iota(jnp.int32, (TILE, LANES), 0).astype(F32).astype(BF16)
    none = jnp.zeros((TILE, LANES), BF16)
    tile_iota = lax.broadcasted_iota(jnp.int32, (TILE, LANES), 0)
    edge_x = (tile_iota // 4).astype(F32).astype(BF16)
    edge_y = (cells_y + tile_iota % 4).astype(F32).astype(BF16)

    def build(q, a_ref, b_ref, slot):
        for member in range(2):
            base = (pair_group[q] + member) * TILE
            first = (slot * 2 + member) * 64

            def row(r, base=base):
                return raw[pl.ds(base + r, 8, stride=0), :]

            def wide(r, base=base):
                return raw[pl.ds(base + r, TILE, stride=0), :].astype(BF16)

            def tap(r, first=first):
                return taps[pl.ds(first + r, TILE, stride=0), :].astype(BF16)

            m = [row(r) for r in range(10)]
            wx, dx, sx = tap_values(row(10), inner)
            x0 = m[0] * wx + m[1] * dx + m[4] * sx
            x1 = m[2] * wx + m[7] * dx
            x2 = m[5] * wx
            x3 = m[3] * wx + m[8] * dx
            x4 = m[9] * wx
            x5 = m[6] * wx
            for half in range(2):
                wy, dy, sy = tap_values(row(11), outer[half])
                taps[first + 8 * half:first + 8 * half + 8, :] = x0 * wy + x1 * dy + x2 * sy
                taps[first + 16 + 8 * half:first + 24 + 8 * half, :] = x3 * wy + x4 * dy
                taps[first + 32 + 8 * half:first + 40 + 8 * half, :] = x5 * wy
            wz, dz, sz = tap_values(row(12), inner)
            taps[first + 48:first + 52, :] = wz[0:4]
            taps[first + 52:first + 56, :] = dz[0:4]
            taps[first + 56:first + 60, :] = sz[0:4]

            zbase = wide(15)
            ztap = [[tap(48 + 4 * k + c) for c in range(4)] for k in range(3)]
            for t in range(NZ // TILE):
                gap = tile_rows + (TILE * t) - zbase
                hit = [gap == c for c in range(4)]
                for k in range(3):
                    value = none
                    for c in range(3, -1, -1):
                        value = jnp.where(hit[c], ztap[k][c], value)
                    b_ref[TILE * t:TILE * (t + 1), (member * 3 + k) * LANES:(member * 3 + k + 1) * LANES] = value
                yield

        for member in range(2):
            base = (pair_group[q] + member) * TILE
            first = (slot * 2 + member) * 64

            def wide(r, base=base):
                return raw[pl.ds(base + r, TILE, stride=0), :].astype(BF16)

            def tap(r, first=first):
                return taps[pl.ds(first + r, TILE, stride=0), :].astype(BF16)

            ybase = wide(14)
            xbase = wide(13)
            gap = edge_y - ybase
            hit = [gap == c for c in range(4)]
            where_x = [[edge_x + 4 * m - xbase == c for c in range(4)] for m in range(3)]
            for k in range(3):
                column = []
                for a in range(4):
                    value = none
                    for b in range(3, -1, -1):
                        value = jnp.where(hit[b], tap(16 * k + 4 * b + a), value)
                    column.append(value)
                for m in range(3):
                    value = none
                    for a in range(3, -1, -1):
                        value = jnp.where(where_x[m][a], column[a], value)
                    a_ref[WIN_X * ROWS_Y + TILE * m:WIN_X * ROWS_Y + TILE * (m + 1),
                          (member * 3 + k) * LANES:(member * 3 + k + 1) * LANES] = value
                yield
            bit2 = xbase >= 4
            xbase = xbase - jnp.where(bit2, jnp.full_like(none, 4), none)
            bit1 = xbase >= 2
            xbase = xbase - jnp.where(bit1, jnp.full_like(none, 2), none)
            bit0 = xbase >= 1
            for t in range(ROWS_Y // TILE):
                gap = tile_rows + (TILE * t) - ybase
                hit = [gap == c for c in range(4)]
                for k in range(3):
                    column = []
                    for a in range(4):
                        value = none
                        for b in range(3, -1, -1):
                            value = jnp.where(hit[b], tap(16 * k + 4 * b + a), value)
                        column.append(value)
                    for bit, step in ((bit0, 1), (bit1, 2), (bit2, 4)):
                        size = len(column)
                        column = [
                            jnp.where(bit, column[i - step] if i >= step else none, column[i] if i < size else none)
                            for i in range(size + step)
                        ]
                    for x in range(WIN_X):
                        a_ref[x * ROWS_Y + TILE * t:x * ROWS_Y + TILE * (t + 1),
                              (member * 3 + k) * LANES:(member * 3 + k + 1) * LANES] = column[x]
                    yield

    def push(b_ref, part, unit, register):
        cut = slice(part * 2 * LANES, (part + 1) * 2 * LANES)
        pltpu.matmul_push_rhs(b_ref[:, cut], register, unit, transpose=True)

    def multiply(sums, a_ref, b_ref):
        def add(part, unit, i, register):
            row, size = CHUNKS[i]
            lhs = a_ref[row:row + size, part * 2 * LANES:(part + 1) * 2 * LANES]
            pltpu.matmul_acc_lhs(sums[unit * len(CHUNKS) + i], lhs, load_staged_rhs=register)

        for i in range(len(CHUNKS)):
            for unit in range(2):
                add(unit, unit, i, None if i else 0)
                yield
            if i < 2:
                push(b_ref, 2, i, 1)
        for i in range(len(CHUNKS) // 2):
            for unit in range(2):
                add(2, unit, i + unit * (len(CHUNKS) // 2), None if i else 1)
                yield

    def flush(sums, plane):
        main = WIN_X * ROWS_Y
        first = pl.multiple_of(plane * (XB * ROWS_Y), XB * ROWS_Y)
        corner = pl.multiple_of(plane * (XB * 4), XB * 4)
        for i, (row, size) in enumerate(CHUNKS):
            part = pltpu.matmul_pop(sums[i]) + pltpu.matmul_pop(sums[len(CHUNKS) + i])
            inside = min(size, main - row)
            for half in range(2):
                cut = slice(half * LANES, (half + 1) * LANES)
                grid, rim = density.at[half], edge.at[half]
                grid[pl.ds(first + row, inside), :] = grid[pl.ds(first + row, inside), :] + part[:inside, cut]
                if inside < size:
                    rim[pl.ds(corner, size - inside), :] = rim[pl.ds(corner, size - inside), :] + part[inside:, cut]

    def step(sums, q, now, later, slot):
        steps = multiply(sums, *now)
        for unit in range(2):
            push(now[1], unit, unit, 0)
        for i, _ in enumerate(build(q + 1, *later, slot)):
            if i >= 2 * BUILD_STEPS and i % BUILD_STEPS == 0:
                next(steps, None)
        for _ in steps:
            pass

        @pl.when(pair_last[q] == 1)
        def _():
            flush(sums, pair_plane[q])

    for _ in build(0, a0, b0, 0):
        pass

    def turns(*sums):
        def turn(i, carry):
            step(sums, 2 * i, (a0, b0), (a1, b1), 1)
            step(sums, 2 * i + 1, (a1, b1), (a0, b0), 0)
            return carry

        lax.fori_loop(0, (pairs + 1) // 2, turn, 0)

    pl.run_scoped(turns, *[pltpu.ACC(unit)((size, NZ), F32) for unit in range(2) for _, size in CHUNKS])

    lines = cells_x + 3
    width = rim_ref.shape[0] // lines
    for half in range(2):
        for y in range(3):
            rim_ref[pl.ds(y * 2 + half, lines, stride=width), :] = edge.at[half][pl.ds(y, lines, stride=4), :]
    for r in range(6, width):
        rim_ref[pl.ds(r, lines, stride=width), :] = jnp.zeros((lines, LANES), F32)


def line_kernel(density_ref, out_ref):
    lines = density_ref.shape[1] // ROWS_Y
    width = out_ref.shape[1] // lines
    columns = width // 2
    for half in range(2):
        for y in range(ROWS_Y):
            out_ref[y // columns, pl.ds(y % columns * 2 + half, lines, stride=width), :] = (
                density_ref.at[half][pl.ds(y, lines, stride=ROWS_Y), :]
            )


def x_kernel(groups, cells_x, in_ref, high_ref, low_ref, out_ref, lines, narrow):
    width = 8
    for l in range(width):
        cut = slice(l * LANES, (l + 1) * LANES)
        for src in range(groups):
            lines[src * cells_x:(src + 1) * cells_x, cut] = in_ref[src, pl.ds(l, cells_x, stride=width), :]
        for src in range(groups):
            first = (src + 1) % groups * cells_x
            lines[first:first + 3, cut] = lines[first:first + 3, cut] + in_ref[src, pl.ds(cells_x * width + l, 3, stride=width), :]
    narrow[...] = lines[...].astype(BF16)
    data = narrow[...]
    result = jnp.dot(high_ref[...], data, preferred_element_type=F32) + jnp.dot(low_ref[...], data, preferred_element_type=F32)
    devices = out_ref.shape[0] // 32
    for q in range(4):
        for l in range(width):
            out_ref[pl.ds(l // 2 * 8 + q * 2 + l % 2, devices, stride=32), :] = (
                result[q * devices:(q + 1) * devices, l * LANES:(l + 1) * LANES]
            )


def y_kernel(per_step, in_ref, high_ref, low_ref, coupling_ref, out_ref, data, spectrum):
    @pl.when(pl.program_id(0) == 0)
    def _():
        half_y = NY // 2
        sums = []
        for odd in range(2):
            for q in range(4):
                for half in range(2):
                    value = in_ref[pl.ds(odd * 8 + q * 2 + half, half_y, stride=16), :]
                    same = slice(q * NZ + half * LANES, q * NZ + (half + 1) * LANES)
                    swap = slice((q ^ 1) * NZ + half * LANES, (q ^ 1) * NZ + (half + 1) * LANES)
                    data[odd, 0:half_y, same] = value.astype(BF16)
                    data[odd, half_y:NY, swap] = (value if q % 2 else -value).astype(BF16)
            lines = data[odd]
            sums.append(
                jnp.dot(high_ref[odd], lines, preferred_element_type=F32)
                + jnp.dot(low_ref[odd], lines, preferred_element_type=F32)
            )
        even, odd = sums
        spectrum[0:half_y, :] = (even + odd).astype(BF16)
        spectrum[half_y:NY, :] = (even - odd).astype(BF16)

    block = NY // MBLK
    dims = (((1,), (1,)), ((), ()))
    for member in range(per_step):
        first = (pl.program_id(0) * per_step + member) * block
        rows = spectrum[pl.ds(pl.multiple_of(first, block), block), :]
        rows = jnp.concatenate([rows[:, q * NZ:(q + 1) * NZ] for q in range(4)], axis=0)
        weight = coupling_ref[member]
        high = weight.astype(BF16)
        low = (weight - high.astype(F32)).astype(BF16)
        result = lax.dot_general(rows, high, dims, preferred_element_type=F32) + lax.dot_general(
            rows, low, dims, preferred_element_type=F32
        )
        for q in range(4):
            out_ref[q % 2, q // 2, member * block:(member + 1) * block, :] = result[q * block:(q + 1) * block]


def two_parts(table):
    high = table.astype(ml_dtypes.bfloat16)
    low = (table - high.astype(np.float64)).astype(ml_dtypes.bfloat16)
    return high, low


def tables(size_x, size_y):
    devices = size_x * size_y
    wave = np.arange(KX).reshape(devices, 2).T.reshape(2, 1, devices, 1)
    angle = 2.0 * np.pi * (wave * np.arange(NX) % NX) / NX
    scale = 1.0 / math.sqrt(NX * NY)
    table_x = np.concatenate([np.cos(angle), -np.sin(angle)], 1).reshape(4 * devices, NX) * scale
    columns = NY // devices
    y = np.arange(size_y)[None, :, None] * (NY // size_y) + np.arange(size_x)[:, None, None] * columns + np.arange(columns)
    y = y.reshape(NY // 2, 2).T.reshape(2, 1, NY // 2)
    angle = 2.0 * np.pi * (np.arange(NY // 2)[None, :, None] * y % NY) / NY
    table_y = np.concatenate([np.cos(angle), np.sin(angle)], 2)
    return two_parts(table_x), two_parts(table_y)


def make_spread(block_count, cells_x, cells_y, size_x):
    lines = cells_x + 3
    groups = block_count + 2 * (cells_x // XB) + 2
    vmem = pltpu.VMEM
    slots = block_count * LANES
    whole = pl.BlockSpec(memory_space=pltpu.VMEM)
    return pl.pallas_call(
        lambda *refs: spread_kernel(cells_x, cells_y, block_count, *refs),
        out_shape=(
            jax.ShapeDtypeStruct((2, lines * ROWS_Y, LANES), F32),
            jax.ShapeDtypeStruct((lines * 8, LANES), F32),
        ),
        in_specs=[pl.BlockSpec(memory_space=pltpu.MemorySpace.HBM)] * 5,
        out_specs=(whole, whole),
        scratch_shapes=[
            pltpu.SMEM((block_count,), jnp.int32),
            pltpu.SMEM((block_count,), jnp.int32),
            vmem((10, slots), F32),
            vmem((3, slots), F32),
            vmem((3, slots), jnp.int32),
            pltpu.SemaphoreType.DMA((5,)),
            vmem((groups * TILE, LANES), F32),
            vmem((256, LANES), F32),
            vmem((ROWS, 6 * LANES), BF16),
            vmem((NZ, 6 * LANES), BF16),
            vmem((ROWS, 6 * LANES), BF16),
            vmem((NZ, 6 * LANES), BF16),
            vmem((2, (lines + 1) * 4, LANES), F32),
            vmem((BATCH, TILE, LANES), F32),
            pltpu.SMEM((8,), jnp.int32),
            pltpu.SMEM((block_count + 16,), jnp.int32),
            pltpu.SMEM((block_count + 16,), jnp.int32),
            pltpu.SMEM((block_count + 16,), jnp.int32),
        ],
        compiler_params=pltpu.CompilerParams(vmem_limit_bytes=20 << 20),
        name="spread",
    )


def make_y(size_x, size_y, per_step):
    devices = size_x * size_y
    _, (y_high, y_low) = tables(size_x, size_y)
    vmem = pltpu.VMEM
    fixed = lambda i: (0, 0)
    call = pl.pallas_call(
        lambda *refs: y_kernel(per_step, *refs),
        out_shape=jax.ShapeDtypeStruct((2, 2, NY, NZ), F32),
        grid=(MBLK // per_step,),
        in_specs=[
            pl.BlockSpec((devices * 32, LANES), fixed, pipeline_mode=pl.Buffered(1)),
            pl.BlockSpec((2, NY // 2, NY), lambda i: (0, 0, 0), pipeline_mode=pl.Buffered(1)),
            pl.BlockSpec((2, NY // 2, NY), lambda i: (0, 0, 0), pipeline_mode=pl.Buffered(1)),
            pl.BlockSpec((per_step, NZ, NZ), lambda i: (i, 0, 0)),
        ],
        out_specs=pl.BlockSpec((2, 2, NY // MBLK * per_step, NZ), lambda i: (0, 0, i, 0)),
        scratch_shapes=[vmem((2, NY, 4 * NZ), BF16), vmem((NY, 4 * NZ), BF16)],
        compiler_params=pltpu.CompilerParams(vmem_limit_bytes=20 << 20),
        name="transform_y",
    )
    return lambda spectrum, coupling: call(spectrum, jnp.asarray(y_high), jnp.asarray(y_low), coupling)


def per_device(multipoles, fractions, base_index, block_plane, atom_count, coupling):
    size_x = lax.axis_size("gx")
    size_y = lax.axis_size("gy")
    cells_x = NX // size_x
    cells_y = NY // size_y
    block_count = block_plane.shape[0]
    devices = size_x * size_y
    (x_high, x_low), _ = tables(size_x, size_y)
    vmem = pltpu.VMEM
    whole = pl.BlockSpec(memory_space=pltpu.VMEM)
    limit = pltpu.CompilerParams(vmem_limit_bytes=20 << 20)

    hbm = pltpu.MemorySpace.HBM
    atoms = (block_plane, atom_count, multipoles, fractions, base_index)
    density, rim = make_spread(block_count, cells_x, cells_y, size_x)(
        *[pltpu.with_memory_space_constraint(array, hbm) for array in atoms]
    )

    rim = lax.ppermute(rim, "gy", [(i, (i + 1) % size_y) for i in range(size_y)])
    density = pl.pallas_call(
        line_kernel,
        out_shape=jax.ShapeDtypeStruct((size_x, (cells_x + 3) * 8, LANES), F32),
        in_specs=[whole],
        out_specs=whole,
        compiler_params=limit,
        name="lines",
    )(density)
    density = density.at[0].add(rim)
    density = lax.all_to_all(density, "gx", split_axis=0, concat_axis=0, tiled=True)

    spectrum = pl.pallas_call(
        lambda *refs: x_kernel(size_x, cells_x, *refs),
        out_shape=jax.ShapeDtypeStruct((devices * 32, LANES), F32),
        in_specs=[whole] * 3,
        out_specs=whole,
        scratch_shapes=[vmem((NX, 8 * LANES), F32), vmem((NX, 8 * LANES), BF16)],
        compiler_params=limit,
        name="transform_x",
    )(density, jnp.asarray(x_high), jnp.asarray(x_low))

    spectrum = lax.all_to_all(
        spectrum.reshape(devices, 32, LANES), ("gx", "gy"), split_axis=0, concat_axis=0, tiled=True
    ).reshape(devices * 32, LANES)

    return make_y(size_x, size_y, 4)(spectrum, coupling)


def solution(mesh):
    return jax.shard_map(
        per_device,
        mesh=mesh,
        in_specs=(
            P(None, ("gx", "gy")),
            P(None, ("gx", "gy")),
            P(None, ("gx", "gy")),
            P(("gx", "gy")),
            P(("gx", "gy")),
            P(),
        ),
        out_specs=P(None, ("gx", "gy"), None, None),
        check_vma=False,
    )
```

```python
import math

import jax
import jax.numpy as jnp
import ml_dtypes
import numpy as np
from jax import lax
from jax.experimental import pallas as pl
from jax.experimental.pallas import tpu as pltpu
from jax.sharding import PartitionSpec as P

NX = 512
NY = 512
NZ = 256
XB = 8
LANES = 128
MBLK = 8
KX = 256
TILE = 16
ROWS_Y = 64
WIN_X = XB + 3
ROWS = WIN_X * ROWS_Y + 3 * TILE
BATCH = 8
BUILD_STEPS = 3
CHUNKS = ((0, 128), (128, 128), (256, 128), (384, 128), (512, 128), (640, 112))
F32 = jnp.float32
BF16 = jnp.bfloat16


def tap_constants(tap):
    def pick(c0, c1, c2, c3):
        return jnp.where(tap == 0, c0, jnp.where(tap == 1, c1, jnp.where(tap == 2, c2, c3))).astype(F32)

    return dict(
        shift=pick(1.0, 0.0, 0.0, 0.0),
        sign=pick(-1.0, 1.0, 1.0, 1.0),
        w=(pick(0.0, 2.0 / 3.0, 1.0 / 6.0, 0.0), pick(0.0, 0.0, 0.5, 0.0), pick(0.0, -1.0, 0.5, 0.0), pick(1.0 / 6.0, 0.5, -0.5, 1.0 / 6.0)),
        d=(pick(0.0, 0.0, 0.5, 0.0), pick(0.0, -2.0, 1.0, 0.0), pick(-0.5, 1.5, -1.5, 0.5)),
        s=(pick(0.0, -2.0, 1.0, 0.0), pick(1.0, 3.0, -3.0, 1.0)),
    )


def tap_values(fraction, const):
    u = const["shift"] + const["sign"] * fraction
    w0, w1, w2, w3 = const["w"]
    d0, d1, d2 = const["d"]
    s0, s1 = const["s"]
    return ((w3 * u + w2) * u + w1) * u + w0, (d2 * u + d1) * u + d0, s1 * u + s0


def spread_kernel(cells_x, cells_y, block_count, plane_in, count_in, moment_in, fraction_in, base_in, density, rim_ref,
                  plane_ref, count_ref, moment_ref, fraction_ref, base_ref, arrived, raw, taps, a0, b0, a1, b1, edge, stage, cursor, pair_group, pair_plane, pair_last):
    planes = cells_x // XB
    room = block_count + 2
    spare = planes * room
    lane = lax.broadcasted_iota(jnp.int32, (TILE, LANES), 1)

    copies = [
        pltpu.make_async_copy(source, target, arrived.at[i])
        for i, (source, target) in enumerate(
            (
                (plane_in, plane_ref),
                (count_in, count_ref),
                (moment_in, moment_ref),
                (fraction_in, fraction_ref),
                (base_in, base_ref),
            )
        )
    ]
    for copy in copies:
        copy.start()
    density[...] = jnp.zeros_like(density)
    edge[...] = jnp.zeros_like(edge)

    copies[0].wait()
    copies[1].wait()

    zero_group = jnp.zeros((TILE, LANES), F32)
    for p in range(planes):
        cursor[p] = p * room * LANES
        raw[p * room * TILE:(p * room + 1) * TILE, :] = zero_group
    for i in range(2):
        raw[(spare + i) * TILE:(spare + i + 1) * TILE, :] = zero_group

    for copy in copies[2:]:
        copy.wait()

    def append(i, carry):
        moved = []
        for k in range(BATCH):
            g = i * BATCH + k
            column = pl.multiple_of(g * LANES, LANES)
            stage[k, 0:10, :] = moment_ref[:, pl.ds(column, LANES)]
            stage[k, 10:13, :] = fraction_ref[:, pl.ds(column, LANES)]
            stage[k, 13:16, :] = base_ref[:, pl.ds(column, LANES)].astype(F32)
        for k in range(BATCH):
            g = i * BATCH + k
            p = plane_ref[g]
            live = count_ref[g]
            place = cursor[p]
            cursor[p] = place + live
            offset = place % LANES
            rows = pltpu.roll(jnp.where(lane < live, stage[k], 0.0), offset, axis=1)
            moved.append((pl.multiple_of(place // LANES * TILE, TILE), lane >= offset, rows))
        for first, keep, rows in moved:
            raw[pl.ds(first, TILE), :] = raw[pl.ds(first, TILE), :] + jnp.where(keep, rows, 0.0)
            raw[pl.ds(first + TILE, TILE), :] = jnp.where(keep, 0.0, rows)
        return carry

    lax.fori_loop(0, block_count // BATCH, append, 0)
    pairs = jnp.int32(0)
    for p in range(planes):
        start = p * room
        after = (cursor[p] + LANES - 1) // LANES
        raw[pl.ds(pl.multiple_of(after * TILE, TILE), TILE), :] = zero_group
        here = (after - start + 1) // 2

        def note(i, carry, start=start, pairs=pairs, here=here, p=p):
            pair_group[pairs + i] = start + 2 * i
            pair_plane[pairs + i] = p
            pair_last[pairs + i] = jnp.where(i == here - 1, 1, 0)
            return carry

        lax.fori_loop(0, here, note, 0)
        pairs = pairs + here
    for i in range(3):
        pair_group[pairs + i] = spare
        pair_plane[pairs + i] = 0
        pair_last[pairs + i] = 1

    sub = lax.broadcasted_iota(jnp.int32, (8, LANES), 0)
    inner = tap_constants(sub % 4)
    outer = [tap_constants(sub // 4), tap_constants(2 + sub // 4)]
    tile_rows = lax.broadcasted_iota(jnp.int32, (TILE, LANES), 0).astype(F32).astype(BF16)
    none = jnp.zeros((TILE, LANES), BF16)
    tile_iota = lax.broadcasted_iota(jnp.int32, (TILE, LANES), 0)
    edge_x = (tile_iota // 4).astype(F32).astype(BF16)
    edge_y = (cells_y + tile_iota % 4).astype(F32).astype(BF16)

    def build(q, a_ref, b_ref, slot):
        for member in range(2):
            base = (pair_group[q] + member) * TILE
            first = (slot * 2 + member) * 64

            def row(r, base=base):
                return raw[pl.ds(base + r, 8, stride=0), :]

            def wide(r, base=base):
                return raw[pl.ds(base + r, TILE, stride=0), :].astype(BF16)

            def tap(r, first=first):
                return taps[pl.ds(first + r, TILE, stride=0), :].astype(BF16)

            m = [row(r) for r in range(10)]
            wx, dx, sx = tap_values(row(10), inner)
            x0 = m[0] * wx + m[1] * dx + m[4] * sx
            x1 = m[2] * wx + m[7] * dx
            x2 = m[5] * wx
            x3 = m[3] * wx + m[8] * dx
            x4 = m[9] * wx
            x5 = m[6] * wx
            for half in range(2):
                wy, dy, sy = tap_values(row(11), outer[half])
                taps[first + 8 * half:first + 8 * half + 8, :] = x0 * wy + x1 * dy + x2 * sy
                taps[first + 16 + 8 * half:first + 24 + 8 * half, :] = x3 * wy + x4 * dy
                taps[first + 32 + 8 * half:first + 40 + 8 * half, :] = x5 * wy
            wz, dz, sz = tap_values(row(12), inner)
            taps[first + 48:first + 52, :] = wz[0:4]
            taps[first + 52:first + 56, :] = dz[0:4]
            taps[first + 56:first + 60, :] = sz[0:4]

            zbase = wide(15)
            ztap = [[tap(48 + 4 * k + c) for c in range(4)] for k in range(3)]
            for t in range(NZ // TILE):
                gap = tile_rows + (TILE * t) - zbase
                hit = [gap == c for c in range(4)]
                for k in range(3):
                    value = none
                    for c in range(3, -1, -1):
                        value = jnp.where(hit[c], ztap[k][c], value)
                    b_ref[TILE * t:TILE * (t + 1), (member * 3 + k) * LANES:(member * 3 + k + 1) * LANES] = value
                yield

        for member in range(2):
            base = (pair_group[q] + member) * TILE
            first = (slot * 2 + member) * 64

            def wide(r, base=base):
                return raw[pl.ds(base + r, TILE, stride=0), :].astype(BF16)

            def tap(r, first=first):
                return taps[pl.ds(first + r, TILE, stride=0), :].astype(BF16)

            ybase = wide(14)
            xbase = wide(13)
            gap = edge_y - ybase
            hit = [gap == c for c in range(4)]
            where_x = [[edge_x + 4 * m - xbase == c for c in range(4)] for m in range(3)]
            for k in range(3):
                column = []
                for a in range(4):
                    value = none
                    for b in range(3, -1, -1):
                        value = jnp.where(hit[b], tap(16 * k + 4 * b + a), value)
                    column.append(value)
                for m in range(3):
                    value = none
                    for a in range(3, -1, -1):
                        value = jnp.where(where_x[m][a], column[a], value)
                    a_ref[WIN_X * ROWS_Y + TILE * m:WIN_X * ROWS_Y + TILE * (m + 1),
                          (member * 3 + k) * LANES:(member * 3 + k + 1) * LANES] = value
                yield
            bit2 = xbase >= 4
            xbase = xbase - jnp.where(bit2, jnp.full_like(none, 4), none)
            bit1 = xbase >= 2
            xbase = xbase - jnp.where(bit1, jnp.full_like(none, 2), none)
            bit0 = xbase >= 1
            for t in range(ROWS_Y // TILE):
                gap = tile_rows + (TILE * t) - ybase
                hit = [gap == c for c in range(4)]
                for k in range(3):
                    column = []
                    for a in range(4):
                        value = none
                        for b in range(3, -1, -1):
                            value = jnp.where(hit[b], tap(16 * k + 4 * b + a), value)
                        column.append(value)
                    for bit, step in ((bit0, 1), (bit1, 2), (bit2, 4)):
                        size = len(column)
                        column = [
                            jnp.where(bit, column[i - step] if i >= step else none, column[i] if i < size else none)
                            for i in range(size + step)
                        ]
                    for x in range(WIN_X):
                        a_ref[x * ROWS_Y + TILE * t:x * ROWS_Y + TILE * (t + 1),
                              (member * 3 + k) * LANES:(member * 3 + k + 1) * LANES] = column[x]
                    yield

    def push(b_ref, part, unit, register):
        cut = slice(part * 2 * LANES, (part + 1) * 2 * LANES)
        pltpu.matmul_push_rhs(b_ref[:, cut], register, unit, transpose=True)

    def multiply(sums, a_ref, b_ref):
        def add(part, unit, i, register):
            row, size = CHUNKS[i]
            lhs = a_ref[row:row + size, part * 2 * LANES:(part + 1) * 2 * LANES]
            pltpu.matmul_acc_lhs(sums[unit * len(CHUNKS) + i], lhs, load_staged_rhs=register)

        for i in range(len(CHUNKS)):
            for unit in range(2):
                add(unit, unit, i, None if i else 0)
                yield
            if i < 2:
                push(b_ref, 2, i, 1)
        for i in range(len(CHUNKS) // 2):
            for unit in range(2):
                add(2, unit, i + unit * (len(CHUNKS) // 2), None if i else 1)
                yield

    def flush(sums, plane):
        main = WIN_X * ROWS_Y
        first = pl.multiple_of(plane * (XB * ROWS_Y), XB * ROWS_Y)
        corner = pl.multiple_of(plane * (XB * 4), XB * 4)
        for i, (row, size) in enumerate(CHUNKS):
            part = pltpu.matmul_pop(sums[i]) + pltpu.matmul_pop(sums[len(CHUNKS) + i])
            inside = min(size, main - row)
            for half in range(2):
                cut = slice(half * LANES, (half + 1) * LANES)
                grid, rim = density.at[half], edge.at[half]
                grid[pl.ds(first + row, inside), :] = grid[pl.ds(first + row, inside), :] + part[:inside, cut]
                if inside < size:
                    rim[pl.ds(corner, size - inside), :] = rim[pl.ds(corner, size - inside), :] + part[inside:, cut]

    def step(sums, q, now, later, slot):
        steps = multiply(sums, *now)
        for unit in range(2):
            push(now[1], unit, unit, 0)
        for i, _ in enumerate(build(q + 1, *later, slot)):
            if i >= 2 * BUILD_STEPS and i % BUILD_STEPS == 0:
                next(steps, None)
        for _ in steps:
            pass

        @pl.when(pair_last[q] == 1)
        def _():
            flush(sums, pair_plane[q])

    for _ in build(0, a0, b0, 0):
        pass

    def turns(*sums):
        def turn(i, carry):
            step(sums, 2 * i, (a0, b0), (a1, b1), 1)
            step(sums, 2 * i + 1, (a1, b1), (a0, b0), 0)
            return carry

        lax.fori_loop(0, (pairs + 1) // 2, turn, 0)

    pl.run_scoped(turns, *[pltpu.ACC(unit)((size, NZ), F32) for unit in range(2) for _, size in CHUNKS])

    lines = cells_x + 3
    width = rim_ref.shape[0] // lines
    for half in range(2):
        for y in range(3):
            rim_ref[pl.ds(y * 2 + half, lines, stride=width), :] = edge.at[half][pl.ds(y, lines, stride=4), :]
    for r in range(6, width):
        rim_ref[pl.ds(r, lines, stride=width), :] = jnp.zeros((lines, LANES), F32)


def line_kernel(density_ref, out_ref):
    lines = density_ref.shape[1] // ROWS_Y
    width = out_ref.shape[1] // lines
    columns = width // 2
    for half in range(2):
        for y in range(ROWS_Y):
            out_ref[y // columns, pl.ds(y % columns * 2 + half, lines, stride=width), :] = (
                density_ref.at[half][pl.ds(y, lines, stride=ROWS_Y), :]
            )


def x_kernel(groups, cells_x, in_ref, table_ref, out_ref, narrow):
    width = 8
    spilled = lax.broadcasted_iota(jnp.int32, (8, LANES), 0) < 3
    for l in range(width):
        cut = slice(l * LANES, (l + 1) * LANES)
        for src in range(groups):
            own = in_ref[src, pl.ds(l, cells_x, stride=width), :]
            last = in_ref[(src - 1) % groups, pl.ds((cells_x - 5) * width + l, 8, stride=width), :]
            spill = jnp.where(spilled, pltpu.roll(last, 3, axis=0), 0.0)
            narrow[src * cells_x:(src + 1) * cells_x, cut] = jnp.concatenate([own[:8] + spill, own[8:]], 0).astype(BF16)
    half = table_ref.shape[0] // 2
    data = narrow[...]
    result = jnp.dot(table_ref[:half], data, preferred_element_type=F32) + jnp.dot(
        table_ref[half:], data, preferred_element_type=F32
    )
    devices = out_ref.shape[0] // 32
    for q in range(4):
        for l in range(width):
            out_ref[pl.ds(l // 2 * 8 + q * 2 + l % 2, devices, stride=32), :] = (
                result[q * devices:(q + 1) * devices, l * LANES:(l + 1) * LANES]
            )


def y_kernel(per_step, in_ref, table_ref, coupling_ref, out_ref, data, spectrum):
    @pl.when(pl.program_id(0) == 0)
    def _():
        half_y = NY // 2
        sums = []
        for odd in range(2):
            for q in range(4):
                for half in range(2):
                    value = in_ref[pl.ds(odd * 8 + q * 2 + half, half_y, stride=16), :]
                    same = slice(q * NZ + half * LANES, q * NZ + (half + 1) * LANES)
                    swap = slice((q ^ 1) * NZ + half * LANES, (q ^ 1) * NZ + (half + 1) * LANES)
                    data[odd, 0:half_y, same] = value.astype(BF16)
                    data[odd, half_y:NY, swap] = (value if q % 2 else -value).astype(BF16)
            sums.append(split_dot(table_ref[odd], data[odd]))
        even, odd = sums
        spectrum[0:half_y, :] = (even + odd).astype(BF16)
        spectrum[half_y:NY, :] = (even - odd).astype(BF16)

    block = NY // MBLK
    dims = (((1,), (1,)), ((), ()))
    for member in range(per_step):
        first = (pl.program_id(0) * per_step + member) * block
        rows = spectrum[pl.ds(pl.multiple_of(first, block), block), :]
        rows = jnp.concatenate([rows[:, q * NZ:(q + 1) * NZ] for q in range(4)], axis=0)
        weight = coupling_ref[member]
        high = weight.astype(BF16)
        low = (weight - high.astype(F32)).astype(BF16)
        result = lax.dot_general(rows, high, dims, preferred_element_type=F32) + lax.dot_general(
            rows, low, dims, preferred_element_type=F32
        )
        for q in range(4):
            out_ref[q % 2, q // 2, member * block:(member + 1) * block, :] = result[q * block:(q + 1) * block]


def two_parts(table):
    high = table.astype(ml_dtypes.bfloat16)
    low = (table - high.astype(np.float64)).astype(ml_dtypes.bfloat16)
    return np.concatenate([high, low], axis=-2)


def split_dot(table, data):
    both = jnp.dot(table, data, preferred_element_type=F32)
    rows = both.shape[0] // 2
    return both[:rows] + both[rows:]


def tables(size_x, size_y):
    devices = size_x * size_y
    wave = np.arange(KX).reshape(devices, 2).T.reshape(2, 1, devices, 1)
    angle = 2.0 * np.pi * (wave * np.arange(NX) % NX) / NX
    scale = 1.0 / math.sqrt(NX * NY)
    table_x = np.concatenate([np.cos(angle), -np.sin(angle)], 1).reshape(4 * devices, NX) * scale
    columns = NY // devices
    y = np.arange(size_y)[None, :, None] * (NY // size_y) + np.arange(size_x)[:, None, None] * columns + np.arange(columns)
    y = y.reshape(NY // 2, 2).T.reshape(2, 1, NY // 2)
    angle = 2.0 * np.pi * (np.arange(NY // 2)[None, :, None] * y % NY) / NY
    table_y = np.concatenate([np.cos(angle), np.sin(angle)], 2)
    return two_parts(table_x), two_parts(table_y)


def make_spread(block_count, cells_x, cells_y, size_x):
    lines = cells_x + 3
    groups = (block_count + 2) * (cells_x // XB) + 2
    vmem = pltpu.VMEM
    slots = block_count * LANES
    whole = pl.BlockSpec(memory_space=pltpu.VMEM)
    return pl.pallas_call(
        lambda *refs: spread_kernel(cells_x, cells_y, block_count, *refs),
        out_shape=(
            jax.ShapeDtypeStruct((2, lines * ROWS_Y, LANES), F32),
            jax.ShapeDtypeStruct((lines * 8, LANES), F32),
        ),
        in_specs=[pl.BlockSpec(memory_space=pltpu.MemorySpace.HBM)] * 5,
        out_specs=(whole, whole),
        scratch_shapes=[
            pltpu.SMEM((block_count,), jnp.int32),
            pltpu.SMEM((block_count,), jnp.int32),
            vmem((10, slots), F32),
            vmem((3, slots), F32),
            vmem((3, slots), jnp.int32),
            pltpu.SemaphoreType.DMA((5,)),
            vmem((groups * TILE, LANES), F32),
            vmem((256, LANES), F32),
            vmem((ROWS, 6 * LANES), BF16),
            vmem((NZ, 6 * LANES), BF16),
            vmem((ROWS, 6 * LANES), BF16),
            vmem((NZ, 6 * LANES), BF16),
            vmem((2, (lines + 1) * 4, LANES), F32),
            vmem((BATCH, TILE, LANES), F32),
            pltpu.SMEM((8,), jnp.int32),
            pltpu.SMEM((block_count + 16,), jnp.int32),
            pltpu.SMEM((block_count + 16,), jnp.int32),
            pltpu.SMEM((block_count + 16,), jnp.int32),
        ],
        compiler_params=pltpu.CompilerParams(vmem_limit_bytes=20 << 20),
        name="spread",
    )


def make_y(size_x, size_y, per_step):
    devices = size_x * size_y
    _, table = tables(size_x, size_y)
    vmem = pltpu.VMEM
    fixed = lambda i: (0, 0)
    call = pl.pallas_call(
        lambda *refs: y_kernel(per_step, *refs),
        out_shape=jax.ShapeDtypeStruct((2, 2, NY, NZ), F32),
        grid=(MBLK // per_step,),
        in_specs=[
            pl.BlockSpec((devices * 32, LANES), fixed, pipeline_mode=pl.Buffered(1)),
            pl.BlockSpec((2, NY, NY), lambda i: (0, 0, 0), pipeline_mode=pl.Buffered(1)),
            pl.BlockSpec((per_step, NZ, NZ), lambda i: (i, 0, 0)),
        ],
        out_specs=pl.BlockSpec((2, 2, NY // MBLK * per_step, NZ), lambda i: (0, 0, i, 0)),
        scratch_shapes=[vmem((2, NY, 4 * NZ), BF16), vmem((NY, 4 * NZ), BF16)],
        compiler_params=pltpu.CompilerParams(vmem_limit_bytes=20 << 20),
        name="transform_y",
    )
    return lambda spectrum, coupling: call(spectrum, jnp.asarray(table), coupling)


def per_device(multipoles, fractions, base_index, block_plane, atom_count, coupling):
    size_x = lax.axis_size("gx")
    size_y = lax.axis_size("gy")
    cells_x = NX // size_x
    cells_y = NY // size_y
    block_count = block_plane.shape[0]
    devices = size_x * size_y
    table, _ = tables(size_x, size_y)
    vmem = pltpu.VMEM
    whole = pl.BlockSpec(memory_space=pltpu.VMEM)
    limit = pltpu.CompilerParams(vmem_limit_bytes=20 << 20)

    hbm = pltpu.MemorySpace.HBM
    atoms = (block_plane, atom_count, multipoles, fractions, base_index)
    density, rim = make_spread(block_count, cells_x, cells_y, size_x)(
        *[pltpu.with_memory_space_constraint(array, hbm) for array in atoms]
    )

    rim = lax.ppermute(rim, "gy", [(i, (i + 1) % size_y) for i in range(size_y)])
    density = pl.pallas_call(
        line_kernel,
        out_shape=jax.ShapeDtypeStruct((size_x, (cells_x + 3) * 8, LANES), F32),
        in_specs=[whole],
        out_specs=whole,
        compiler_params=limit,
        name="lines",
    )(density)
    density = density.at[0].add(rim)
    density = lax.all_to_all(density, "gx", split_axis=0, concat_axis=0, tiled=True)

    spectrum = pl.pallas_call(
        lambda *refs: x_kernel(size_x, cells_x, *refs),
        out_shape=jax.ShapeDtypeStruct((devices * 32, LANES), F32),
        in_specs=[whole] * 2,
        out_specs=whole,
        scratch_shapes=[vmem((NX, 8 * LANES), BF16)],
        compiler_params=limit,
        name="transform_x",
    )(density, jnp.asarray(table))

    spectrum = lax.all_to_all(
        spectrum.reshape(devices, 32, LANES), ("gx", "gy"), split_axis=0, concat_axis=0, tiled=True
    ).reshape(devices * 32, LANES)

    return make_y(size_x, size_y, 4)(spectrum, coupling)


def solution(mesh):
    return jax.shard_map(
        per_device,
        mesh=mesh,
        in_specs=(
            P(None, ("gx", "gy")),
            P(None, ("gx", "gy")),
            P(None, ("gx", "gy")),
            P(("gx", "gy")),
            P(("gx", "gy")),
            P(),
        ),
        out_specs=P(None, ("gx", "gy"), None, None),
        check_vma=False,
    )
```

```python
import math

import jax
import jax.numpy as jnp
import ml_dtypes
import numpy as np
from jax import lax
from jax.experimental import pallas as pl
from jax.experimental.pallas import tpu as pltpu
from jax.sharding import PartitionSpec as P

NX = 512
NY = 512
NZ = 256
XB = 8
LANES = 128
MBLK = 8
KX = 256
TILE = 16
ROWS_Y = 64
WIN_X = XB + 3
ROWS = WIN_X * ROWS_Y + 3 * TILE
BATCH = 8
BUILD_STEPS = 3
CHUNKS = ((0, 128), (128, 128), (256, 128), (384, 128), (512, 128), (640, 112))
F32 = jnp.float32
BF16 = jnp.bfloat16


def tap_constants(tap):
    def pick(c0, c1, c2, c3):
        return jnp.where(tap == 0, c0, jnp.where(tap == 1, c1, jnp.where(tap == 2, c2, c3))).astype(F32)

    return dict(
        shift=pick(1.0, 0.0, 0.0, 0.0),
        sign=pick(-1.0, 1.0, 1.0, 1.0),
        w=(pick(0.0, 2.0 / 3.0, 1.0 / 6.0, 0.0), pick(0.0, 0.0, 0.5, 0.0), pick(0.0, -1.0, 0.5, 0.0), pick(1.0 / 6.0, 0.5, -0.5, 1.0 / 6.0)),
        d=(pick(0.0, 0.0, 0.5, 0.0), pick(0.0, -2.0, 1.0, 0.0), pick(-0.5, 1.5, -1.5, 0.5)),
        s=(pick(0.0, -2.0, 1.0, 0.0), pick(1.0, 3.0, -3.0, 1.0)),
    )


def tap_values(fraction, const):
    u = const["shift"] + const["sign"] * fraction
    w0, w1, w2, w3 = const["w"]
    d0, d1, d2 = const["d"]
    s0, s1 = const["s"]
    return ((w3 * u + w2) * u + w1) * u + w0, (d2 * u + d1) * u + d0, s1 * u + s0


def spread_kernel(cells_x, cells_y, block_count, plane_in, count_in, moment_in, fraction_in, base_in, density, rim_ref,
                  plane_ref, count_ref, moment_ref, fraction_ref, base_ref, arrived, raw, taps, a0, b0, a1, b1, edge, stage, cursor, pair_group, pair_plane, pair_last):
    planes = cells_x // XB
    room = block_count + 2
    spare = planes * room
    lane = lax.broadcasted_iota(jnp.int32, (TILE, LANES), 1)

    copies = [
        pltpu.make_async_copy(source, target, arrived.at[i])
        for i, (source, target) in enumerate(
            (
                (plane_in, plane_ref),
                (count_in, count_ref),
                (moment_in, moment_ref),
                (fraction_in, fraction_ref),
                (base_in, base_ref),
            )
        )
    ]
    for copy in copies:
        copy.start()
    density[...] = jnp.zeros_like(density)
    edge[...] = jnp.zeros_like(edge)

    copies[0].wait()
    copies[1].wait()

    zero_group = jnp.zeros((TILE, LANES), F32)
    for p in range(planes):
        cursor[p] = p * room * LANES
        raw[p * room * TILE:(p * room + 1) * TILE, :] = zero_group
    for i in range(2):
        raw[(spare + i) * TILE:(spare + i + 1) * TILE, :] = zero_group

    for copy in copies[2:]:
        copy.wait()

    def append(i, carry):
        moved = []
        for k in range(BATCH):
            g = i * BATCH + k
            column = pl.multiple_of(g * LANES, LANES)
            stage[k, 0:10, :] = moment_ref[:, pl.ds(column, LANES)]
            stage[k, 10:13, :] = fraction_ref[:, pl.ds(column, LANES)]
            stage[k, 13:16, :] = base_ref[:, pl.ds(column, LANES)].astype(F32)
        for k in range(BATCH):
            g = i * BATCH + k
            p = plane_ref[g]
            live = count_ref[g]
            place = cursor[p]
            cursor[p] = place + live
            offset = place % LANES
            rows = pltpu.roll(jnp.where(lane < live, stage[k], 0.0), offset, axis=1)
            moved.append((pl.multiple_of(place // LANES * TILE, TILE), lane >= offset, rows))
        for first, keep, rows in moved:
            raw[pl.ds(first, TILE), :] = raw[pl.ds(first, TILE), :] + jnp.where(keep, rows, 0.0)
            raw[pl.ds(first + TILE, TILE), :] = jnp.where(keep, 0.0, rows)
        return carry

    lax.fori_loop(0, block_count // BATCH, append, 0)
    pairs = jnp.int32(0)
    for p in range(planes):
        start = p * room
        after = (cursor[p] + LANES - 1) // LANES
        raw[pl.ds(pl.multiple_of(after * TILE, TILE), TILE), :] = zero_group
        here = (after - start + 1) // 2

        def note(i, carry, start=start, pairs=pairs, here=here, p=p):
            pair_group[pairs + i] = start + 2 * i
            pair_plane[pairs + i] = p
            pair_last[pairs + i] = jnp.where(i == here - 1, 1, 0)
            return carry

        lax.fori_loop(0, here, note, 0)
        pairs = pairs + here
    for i in range(3):
        pair_group[pairs + i] = spare
        pair_plane[pairs + i] = 0
        pair_last[pairs + i] = 1

    sub = lax.broadcasted_iota(jnp.int32, (8, LANES), 0)
    inner = tap_constants(sub % 4)
    outer = [tap_constants(sub // 4), tap_constants(2 + sub // 4)]
    tile_rows = lax.broadcasted_iota(jnp.int32, (TILE, LANES), 0).astype(F32).astype(BF16)
    none = jnp.zeros((TILE, LANES), BF16)
    tile_iota = lax.broadcasted_iota(jnp.int32, (TILE, LANES), 0)
    edge_x = (tile_iota // 4).astype(F32).astype(BF16)
    edge_y = (cells_y + tile_iota % 4).astype(F32).astype(BF16)

    def build(q, a_ref, b_ref, slot):
        for member in range(2):
            base = (pair_group[q] + member) * TILE
            first = (slot * 2 + member) * 64

            def row(r, base=base):
                return raw[pl.ds(base + r, 8, stride=0), :]

            def wide(r, base=base):
                return raw[pl.ds(base + r, TILE, stride=0), :].astype(BF16)

            def tap(r, first=first):
                return taps[pl.ds(first + r, TILE, stride=0), :].astype(BF16)

            m = [row(r) for r in range(10)]
            wx, dx, sx = tap_values(row(10), inner)
            x0 = m[0] * wx + m[1] * dx + m[4] * sx
            x1 = m[2] * wx + m[7] * dx
            x2 = m[5] * wx
            x3 = m[3] * wx + m[8] * dx
            x4 = m[9] * wx
            x5 = m[6] * wx
            for half in range(2):
                wy, dy, sy = tap_values(row(11), outer[half])
                taps[first + 8 * half:first + 8 * half + 8, :] = x0 * wy + x1 * dy + x2 * sy
                taps[first + 16 + 8 * half:first + 24 + 8 * half, :] = x3 * wy + x4 * dy
                taps[first + 32 + 8 * half:first + 40 + 8 * half, :] = x5 * wy
            wz, dz, sz = tap_values(row(12), inner)
            taps[first + 48:first + 52, :] = wz[0:4]
            taps[first + 52:first + 56, :] = dz[0:4]
            taps[first + 56:first + 60, :] = sz[0:4]

            zbase = wide(15)
            ztap = [[tap(48 + 4 * k + c) for c in range(4)] for k in range(3)]
            for t in range(NZ // TILE):
                gap = tile_rows + (TILE * t) - zbase
                hit = [gap == c for c in range(4)]
                for k in range(3):
                    value = none
                    for c in range(3, -1, -1):
                        value = jnp.where(hit[c], ztap[k][c], value)
                    b_ref[TILE * t:TILE * (t + 1), (member * 3 + k) * LANES:(member * 3 + k + 1) * LANES] = value
                yield

        for member in range(2):
            base = (pair_group[q] + member) * TILE
            first = (slot * 2 + member) * 64

            def wide(r, base=base):
                return raw[pl.ds(base + r, TILE, stride=0), :].astype(BF16)

            def tap(r, first=first):
                return taps[pl.ds(first + r, TILE, stride=0), :].astype(BF16)

            ybase = wide(14)
            xbase = wide(13)
            gap = edge_y - ybase
            hit = [gap == c for c in range(4)]
            where_x = [[edge_x + 4 * m - xbase == c for c in range(4)] for m in range(3)]
            for k in range(3):
                column = []
                for a in range(4):
                    value = none
                    for b in range(3, -1, -1):
                        value = jnp.where(hit[b], tap(16 * k + 4 * b + a), value)
                    column.append(value)
                for m in range(3):
                    value = none
                    for a in range(3, -1, -1):
                        value = jnp.where(where_x[m][a], column[a], value)
                    a_ref[WIN_X * ROWS_Y + TILE * m:WIN_X * ROWS_Y + TILE * (m + 1),
                          (member * 3 + k) * LANES:(member * 3 + k + 1) * LANES] = value
                yield
            bit2 = xbase >= 4
            xbase = xbase - jnp.where(bit2, jnp.full_like(none, 4), none)
            bit1 = xbase >= 2
            xbase = xbase - jnp.where(bit1, jnp.full_like(none, 2), none)
            bit0 = xbase >= 1
            for t in range(ROWS_Y // TILE):
                gap = tile_rows + (TILE * t) - ybase
                hit = [gap == c for c in range(4)]
                for k in range(3):
                    column = []
                    for a in range(4):
                        value = none
                        for b in range(3, -1, -1):
                            value = jnp.where(hit[b], tap(16 * k + 4 * b + a), value)
                        column.append(value)
                    for bit, step in ((bit0, 1), (bit1, 2), (bit2, 4)):
                        size = len(column)
                        column = [
                            jnp.where(bit, column[i - step] if i >= step else none, column[i] if i < size else none)
                            for i in range(size + step)
                        ]
                    for x in range(WIN_X):
                        a_ref[x * ROWS_Y + TILE * t:x * ROWS_Y + TILE * (t + 1),
                              (member * 3 + k) * LANES:(member * 3 + k + 1) * LANES] = column[x]
                    yield

    def push(b_ref, part, unit, register):
        cut = slice(part * 2 * LANES, (part + 1) * 2 * LANES)
        pltpu.matmul_push_rhs(b_ref[:, cut], register, unit, transpose=True)

    def multiply(sums, a_ref, b_ref):
        def add(part, unit, i, register):
            row, size = CHUNKS[i]
            lhs = a_ref[row:row + size, part * 2 * LANES:(part + 1) * 2 * LANES]
            pltpu.matmul_acc_lhs(sums[unit * len(CHUNKS) + i], lhs, load_staged_rhs=register)

        for i in range(len(CHUNKS)):
            for unit in range(2):
                add(unit, unit, i, None if i else 0)
                yield
            if i < 2:
                push(b_ref, 2, i, 1)
        for i in range(len(CHUNKS) // 2):
            for unit in range(2):
                add(2, unit, i + unit * (len(CHUNKS) // 2), None if i else 1)
                yield

    def flush(sums, plane):
        main = WIN_X * ROWS_Y
        first = pl.multiple_of(plane * (XB * ROWS_Y), XB * ROWS_Y)
        corner = pl.multiple_of(plane * (XB * 4), XB * 4)
        for i, (row, size) in enumerate(CHUNKS):
            part = pltpu.matmul_pop(sums[i]) + pltpu.matmul_pop(sums[len(CHUNKS) + i])
            inside = min(size, main - row)
            for half in range(2):
                cut = slice(half * LANES, (half + 1) * LANES)
                grid, rim = density.at[half], edge.at[half]
                grid[pl.ds(first + row, inside), :] = grid[pl.ds(first + row, inside), :] + part[:inside, cut]
                if inside < size:
                    rim[pl.ds(corner, size - inside), :] = rim[pl.ds(corner, size - inside), :] + part[inside:, cut]

    def step(sums, q, now, later, slot):
        steps = multiply(sums, *now)
        for unit in range(2):
            push(now[1], unit, unit, 0)
        for i, _ in enumerate(build(q + 1, *later, slot)):
            if i >= 2 * BUILD_STEPS and i % BUILD_STEPS == 0:
                next(steps, None)
        for _ in steps:
            pass

        @pl.when(pair_last[q] == 1)
        def _():
            flush(sums, pair_plane[q])

    for _ in build(0, a0, b0, 0):
        pass

    def turns(*sums):
        def turn(i, carry):
            step(sums, 2 * i, (a0, b0), (a1, b1), 1)
            step(sums, 2 * i + 1, (a1, b1), (a0, b0), 0)
            return carry

        lax.fori_loop(0, (pairs + 1) // 2, turn, 0)

    pl.run_scoped(turns, *[pltpu.ACC(unit)((size, NZ), F32) for unit in range(2) for _, size in CHUNKS])

    lines = cells_x + 3
    width = rim_ref.shape[0] // lines
    for half in range(2):
        for y in range(3):
            rim_ref[pl.ds(y * 2 + half, lines, stride=width), :] = edge.at[half][pl.ds(y, lines, stride=4), :]
    for r in range(6, width):
        rim_ref[pl.ds(r, lines, stride=width), :] = jnp.zeros((lines, LANES), F32)


def line_kernel(density_ref, out_ref):
    lines = density_ref.shape[1] // ROWS_Y
    width = out_ref.shape[1] // lines
    columns = width // 2
    for half in range(2):
        for y in range(ROWS_Y):
            out_ref[y // columns, pl.ds(y % columns * 2 + half, lines, stride=width), :] = (
                density_ref.at[half][pl.ds(y, lines, stride=ROWS_Y), :]
            )


def x_kernel(groups, cells_x, in_ref, table_ref, out_ref, narrow):
    width = 8
    spilled = lax.broadcasted_iota(jnp.int32, (8, LANES), 0) < 3
    for l in range(width):
        cut = slice(l * LANES, (l + 1) * LANES)
        for src in range(groups):
            own = in_ref[src, pl.ds(l, cells_x, stride=width), :]
            last = in_ref[(src - 1) % groups, pl.ds((cells_x - 5) * width + l, 8, stride=width), :]
            spill = jnp.where(spilled, pltpu.roll(last, 3, axis=0), 0.0)
            narrow[src * cells_x:(src + 1) * cells_x, cut] = jnp.concatenate([own[:8] + spill, own[8:]], 0).astype(BF16)
    half = table_ref.shape[0] // 2
    data = narrow[...]
    result = jnp.dot(table_ref[:half], data, preferred_element_type=F32) + jnp.dot(
        table_ref[half:], data, preferred_element_type=F32
    )
    devices = out_ref.shape[0] // 32
    for q in range(4):
        for l in range(width):
            out_ref[pl.ds(l // 2 * 8 + q * 2 + l % 2, devices, stride=32), :] = (
                result[q * devices:(q + 1) * devices, l * LANES:(l + 1) * LANES]
            )


def y_kernel(per_step, in_ref, table_ref, coupling_ref, out_ref, data, spectrum):
    @pl.when(pl.program_id(0) == 0)
    def _():
        half_y = NY // 2
        sums = []
        for odd in range(2):
            for q in range(4):
                for half in range(2):
                    value = in_ref[pl.ds(odd * 8 + q * 2 + half, half_y, stride=16), :]
                    same = slice(q * NZ + half * LANES, q * NZ + (half + 1) * LANES)
                    swap = slice((q ^ 1) * NZ + half * LANES, (q ^ 1) * NZ + (half + 1) * LANES)
                    data[odd, 0:half_y, same] = value.astype(BF16)
                    data[odd, half_y:NY, swap] = (value if q % 2 else -value).astype(BF16)
            sums.append(split_dot(table_ref[odd], data[odd]))
        even, odd = sums
        spectrum[0:half_y, :] = (even + odd).astype(BF16)
        spectrum[half_y:NY, :] = (even - odd).astype(BF16)

    block = NY // MBLK
    dims = (((1,), (1,)), ((), ()))
    for member in range(per_step):
        first = (pl.program_id(0) * per_step + member) * block
        rows = spectrum[pl.ds(pl.multiple_of(first, block), block), :]
        rows = jnp.concatenate([rows[:, q * NZ:(q + 1) * NZ] for q in range(4)], axis=0)
        weight = coupling_ref[member]
        high = weight.astype(BF16)
        low = (weight - high.astype(F32)).astype(BF16)
        result = lax.dot_general(rows, high, dims, preferred_element_type=F32) + lax.dot_general(
            rows, low, dims, preferred_element_type=F32
        )
        for q in range(4):
            out_ref[q % 2, q // 2, member * block:(member + 1) * block, :] = result[q * block:(q + 1) * block]


def two_parts(table):
    high = table.astype(ml_dtypes.bfloat16)
    low = (table - high.astype(np.float64)).astype(ml_dtypes.bfloat16)
    return np.concatenate([high, low], axis=-2)


def split_dot(table, data):
    both = jnp.dot(table, data, preferred_element_type=F32)
    rows = both.shape[0] // 2
    return both[:rows] + both[rows:]


def tables(size_x, size_y):
    devices = size_x * size_y
    wave = np.arange(KX).reshape(devices, 2).T.reshape(2, 1, devices, 1)
    angle = 2.0 * np.pi * (wave * np.arange(NX) % NX) / NX
    scale = 1.0 / math.sqrt(NX * NY)
    table_x = np.concatenate([np.cos(angle), -np.sin(angle)], 1).reshape(4 * devices, NX) * scale
    columns = NY // devices
    y = np.arange(size_y)[None, :, None] * (NY // size_y) + np.arange(size_x)[:, None, None] * columns + np.arange(columns)
    y = y.reshape(NY // 2, 2).T.reshape(2, 1, NY // 2)
    angle = 2.0 * np.pi * (np.arange(NY // 2)[None, :, None] * y % NY) / NY
    table_y = np.concatenate([np.cos(angle), np.sin(angle)], 2)
    return two_parts(table_x), two_parts(table_y)


def make_spread(block_count, cells_x, cells_y, size_x):
    lines = cells_x + 3
    groups = (block_count + 2) * (cells_x // XB) + 3
    vmem = pltpu.VMEM
    slots = block_count * LANES
    whole = pl.BlockSpec(memory_space=pltpu.VMEM)
    return pl.pallas_call(
        lambda *refs: spread_kernel(cells_x, cells_y, block_count, *refs),
        out_shape=(
            jax.ShapeDtypeStruct((2, lines * ROWS_Y, LANES), F32),
            jax.ShapeDtypeStruct((lines * 8, LANES), F32),
        ),
        in_specs=[pl.BlockSpec(memory_space=pltpu.MemorySpace.HBM)] * 5,
        out_specs=(whole, whole),
        scratch_shapes=[
            pltpu.SMEM((block_count,), jnp.int32),
            pltpu.SMEM((block_count,), jnp.int32),
            vmem((10, slots), F32),
            vmem((3, slots), F32),
            vmem((3, slots), jnp.int32),
            pltpu.SemaphoreType.DMA((5,)),
            vmem((groups * TILE, LANES), F32),
            vmem((256 + TILE, LANES), F32),
            vmem((ROWS, 6 * LANES), BF16),
            vmem((NZ, 6 * LANES), BF16),
            vmem((ROWS, 6 * LANES), BF16),
            vmem((NZ, 6 * LANES), BF16),
            vmem((2, (lines + 1) * 4, LANES), F32),
            vmem((BATCH, TILE, LANES), F32),
            pltpu.SMEM((8,), jnp.int32),
            pltpu.SMEM((block_count + 16,), jnp.int32),
            pltpu.SMEM((block_count + 16,), jnp.int32),
            pltpu.SMEM((block_count + 16,), jnp.int32),
        ],
        compiler_params=pltpu.CompilerParams(vmem_limit_bytes=20 << 20),
        name="spread",
    )


def make_y(size_x, size_y, per_step):
    devices = size_x * size_y
    _, table = tables(size_x, size_y)
    vmem = pltpu.VMEM
    fixed = lambda i: (0, 0)
    call = pl.pallas_call(
        lambda *refs: y_kernel(per_step, *refs),
        out_shape=jax.ShapeDtypeStruct((2, 2, NY, NZ), F32),
        grid=(MBLK // per_step,),
        in_specs=[
            pl.BlockSpec((devices * 32, LANES), fixed, pipeline_mode=pl.Buffered(1)),
            pl.BlockSpec((2, NY, NY), lambda i: (0, 0, 0), pipeline_mode=pl.Buffered(1)),
            pl.BlockSpec((per_step, NZ, NZ), lambda i: (i, 0, 0)),
        ],
        out_specs=pl.BlockSpec((2, 2, NY // MBLK * per_step, NZ), lambda i: (0, 0, i, 0)),
        scratch_shapes=[vmem((2, NY, 4 * NZ), BF16), vmem((NY, 4 * NZ), BF16)],
        compiler_params=pltpu.CompilerParams(vmem_limit_bytes=20 << 20),
        name="transform_y",
    )
    return lambda spectrum, coupling: call(spectrum, jnp.asarray(table), coupling)


def per_device(multipoles, fractions, base_index, block_plane, atom_count, coupling):
    size_x = lax.axis_size("gx")
    size_y = lax.axis_size("gy")
    cells_x = NX // size_x
    cells_y = NY // size_y
    block_count = block_plane.shape[0]
    devices = size_x * size_y
    table, _ = tables(size_x, size_y)
    vmem = pltpu.VMEM
    whole = pl.BlockSpec(memory_space=pltpu.VMEM)
    limit = pltpu.CompilerParams(vmem_limit_bytes=20 << 20)

    hbm = pltpu.MemorySpace.HBM
    atoms = (block_plane, atom_count, multipoles, fractions, base_index)
    density, rim = make_spread(block_count, cells_x, cells_y, size_x)(
        *[pltpu.with_memory_space_constraint(array, hbm) for array in atoms]
    )

    rim = lax.ppermute(rim, "gy", [(i, (i + 1) % size_y) for i in range(size_y)])
    density = pl.pallas_call(
        line_kernel,
        out_shape=jax.ShapeDtypeStruct((size_x, (cells_x + 3) * 8, LANES), F32),
        in_specs=[whole],
        out_specs=whole,
        compiler_params=limit,
        name="lines",
    )(density)
    density = density.at[0].add(rim)
    density = lax.all_to_all(density, "gx", split_axis=0, concat_axis=0, tiled=True)

    spectrum = pl.pallas_call(
        lambda *refs: x_kernel(size_x, cells_x, *refs),
        out_shape=jax.ShapeDtypeStruct((devices * 32, LANES), F32),
        in_specs=[whole] * 2,
        out_specs=whole,
        scratch_shapes=[vmem((NX, 8 * LANES), BF16)],
        compiler_params=limit,
        name="transform_x",
    )(density, jnp.asarray(table))

    spectrum = lax.all_to_all(
        spectrum.reshape(devices, 32, LANES), ("gx", "gy"), split_axis=0, concat_axis=0, tiled=True
    ).reshape(devices * 32, LANES)

    return make_y(size_x, size_y, 4)(spectrum, coupling)


def solution(mesh):
    return jax.shard_map(
        per_device,
        mesh=mesh,
        in_specs=(
            P(None, ("gx", "gy")),
            P(None, ("gx", "gy")),
            P(None, ("gx", "gy")),
            P(("gx", "gy")),
            P(("gx", "gy")),
            P(),
        ),
        out_specs=P(None, ("gx", "gy"), None, None),
        check_vma=False,
    )
```

```python
import math

import jax
import jax.numpy as jnp
import ml_dtypes
import numpy as np
from jax import lax
from jax.experimental import pallas as pl
from jax.experimental.pallas import tpu as pltpu
from jax.sharding import PartitionSpec as P

NX = 512
NY = 512
NZ = 256
XB = 8
LANES = 128
MBLK = 8
KX = 256
TILE = 16
ROWS_Y = 64
WIN_X = XB + 3
ROWS = WIN_X * ROWS_Y + 3 * TILE
BATCH = 8
BUILD_STEPS = 3
CHUNKS = ((0, 128), (128, 128), (256, 128), (384, 128), (512, 128), (640, 112))
F32 = jnp.float32
BF16 = jnp.bfloat16


def tap_constants(tap):
    def pick(c0, c1, c2, c3):
        return jnp.where(tap == 0, c0, jnp.where(tap == 1, c1, jnp.where(tap == 2, c2, c3))).astype(F32)

    return dict(
        shift=pick(1.0, 0.0, 0.0, 0.0),
        sign=pick(-1.0, 1.0, 1.0, 1.0),
        w=(pick(0.0, 2.0 / 3.0, 1.0 / 6.0, 0.0), pick(0.0, 0.0, 0.5, 0.0), pick(0.0, -1.0, 0.5, 0.0), pick(1.0 / 6.0, 0.5, -0.5, 1.0 / 6.0)),
        d=(pick(0.0, 0.0, 0.5, 0.0), pick(0.0, -2.0, 1.0, 0.0), pick(-0.5, 1.5, -1.5, 0.5)),
        s=(pick(0.0, -2.0, 1.0, 0.0), pick(1.0, 3.0, -3.0, 1.0)),
    )


def tap_values(fraction, const):
    u = const["shift"] + const["sign"] * fraction
    w0, w1, w2, w3 = const["w"]
    d0, d1, d2 = const["d"]
    s0, s1 = const["s"]
    return ((w3 * u + w2) * u + w1) * u + w0, (d2 * u + d1) * u + d0, s1 * u + s0


def spread_kernel(cells_x, cells_y, block_count, plane_in, count_in, moment_in, fraction_in, base_in, density, rim_ref,
                  plane_ref, count_ref, moment_ref, fraction_ref, base_ref, arrived, raw, taps, a0, b0, a1, b1, edge, stage, cursor, pair_group, pair_plane, pair_last):
    planes = cells_x // XB
    room = block_count + 2
    spare = planes * room
    lane = lax.broadcasted_iota(jnp.int32, (TILE, LANES), 1)

    copies = [
        pltpu.make_async_copy(source, target, arrived.at[i])
        for i, (source, target) in enumerate(
            (
                (plane_in, plane_ref),
                (count_in, count_ref),
                (moment_in, moment_ref),
                (fraction_in, fraction_ref),
                (base_in, base_ref),
            )
        )
    ]
    for copy in copies:
        copy.start()
    density[...] = jnp.zeros_like(density)
    edge[...] = jnp.zeros_like(edge)

    copies[0].wait()
    copies[1].wait()

    zero_group = jnp.zeros((TILE, LANES), F32)
    for p in range(planes):
        cursor[p] = p * room * LANES
        raw[p * room * TILE:(p * room + 1) * TILE, :] = zero_group
    for i in range(2):
        raw[(spare + i) * TILE:(spare + i + 1) * TILE, :] = zero_group

    for copy in copies[2:]:
        copy.wait()

    def append(i, carry):
        moved = []
        for k in range(BATCH):
            g = i * BATCH + k
            column = pl.multiple_of(g * LANES, LANES)
            stage[k, 0:10, :] = moment_ref[:, pl.ds(column, LANES)]
            stage[k, 10:13, :] = fraction_ref[:, pl.ds(column, LANES)]
            stage[k, 13:16, :] = base_ref[:, pl.ds(column, LANES)].astype(F32)
        for k in range(BATCH):
            g = i * BATCH + k
            p = plane_ref[g]
            live = count_ref[g]
            place = cursor[p]
            cursor[p] = place + live
            offset = place % LANES
            rows = pltpu.roll(jnp.where(lane < live, stage[k], 0.0), offset, axis=1)
            moved.append((pl.multiple_of(place // LANES * TILE, TILE), lane >= offset, rows))
        for first, keep, rows in moved:
            raw[pl.ds(first, TILE), :] = raw[pl.ds(first, TILE), :] + jnp.where(keep, rows, 0.0)
            raw[pl.ds(first + TILE, TILE), :] = jnp.where(keep, 0.0, rows)
        return carry

    lax.fori_loop(0, block_count // BATCH, append, 0)
    pairs = jnp.int32(0)
    for p in range(planes):
        start = p * room
        after = (cursor[p] + LANES - 1) // LANES
        raw[pl.ds(pl.multiple_of(after * TILE, TILE), TILE), :] = zero_group
        here = (after - start + 1) // 2

        def note(i, carry, start=start, pairs=pairs, here=here, p=p):
            pair_group[pairs + i] = start + 2 * i
            pair_plane[pairs + i] = p
            pair_last[pairs + i] = jnp.where(i == here - 1, 1, 0)
            return carry

        lax.fori_loop(0, here, note, 0)
        pairs = pairs + here
    for i in range(3):
        pair_group[pairs + i] = spare
        pair_plane[pairs + i] = 0
        pair_last[pairs + i] = 1

    sub = lax.broadcasted_iota(jnp.int32, (8, LANES), 0)
    inner = tap_constants(sub % 4)
    outer = [tap_constants(sub // 4), tap_constants(2 + sub // 4)]
    tile_rows = lax.broadcasted_iota(jnp.int32, (TILE, LANES), 0).astype(F32).astype(BF16)
    none = jnp.zeros((TILE, LANES), BF16)
    tile_iota = lax.broadcasted_iota(jnp.int32, (TILE, LANES), 0)
    edge_x = (tile_iota // 4).astype(F32).astype(BF16)
    edge_y = (cells_y + tile_iota % 4).astype(F32).astype(BF16)

    def build(q, a_ref, b_ref, slot):
        for member in range(2):
            base = (pair_group[q] + member) * TILE
            first = (slot * 2 + member) * 64

            def row(r, base=base):
                return raw[pl.ds(base + r, 8, stride=0), :]

            def wide(r, base=base):
                return raw[pl.ds(base + r, TILE, stride=0), :].astype(BF16)

            def tap(r, first=first):
                return taps[pl.ds(first + r, TILE, stride=0), :].astype(BF16)

            m = [row(r) for r in range(10)]
            wx, dx, sx = tap_values(row(10), inner)
            x0 = m[0] * wx + m[1] * dx + m[4] * sx
            x1 = m[2] * wx + m[7] * dx
            x2 = m[5] * wx
            x3 = m[3] * wx + m[8] * dx
            x4 = m[9] * wx
            x5 = m[6] * wx
            for half in range(2):
                wy, dy, sy = tap_values(row(11), outer[half])
                taps[first + 8 * half:first + 8 * half + 8, :] = x0 * wy + x1 * dy + x2 * sy
                taps[first + 16 + 8 * half:first + 24 + 8 * half, :] = x3 * wy + x4 * dy
                taps[first + 32 + 8 * half:first + 40 + 8 * half, :] = x5 * wy
            wz, dz, sz = tap_values(row(12), inner)
            taps[first + 48:first + 52, :] = wz[0:4]
            taps[first + 52:first + 56, :] = dz[0:4]
            taps[first + 56:first + 60, :] = sz[0:4]

            zbase = wide(15)
            ztap = [[tap(48 + 4 * k + c) for c in range(4)] for k in range(3)]
            for t in range(NZ // TILE):
                gap = tile_rows + (TILE * t) - zbase
                hit = [gap == c for c in range(4)]
                for k in range(3):
                    value = none
                    for c in range(3, -1, -1):
                        value = jnp.where(hit[c], ztap[k][c], value)
                    b_ref[TILE * t:TILE * (t + 1), (member * 3 + k) * LANES:(member * 3 + k + 1) * LANES] = value
                yield

        for member in range(2):
            base = (pair_group[q] + member) * TILE
            first = (slot * 2 + member) * 64

            def wide(r, base=base):
                return raw[pl.ds(base + r, TILE, stride=0), :].astype(BF16)

            def tap(r, first=first):
                return taps[pl.ds(first + r, TILE, stride=0), :].astype(BF16)

            ybase = wide(14)
            xbase = wide(13)
            gap = edge_y - ybase
            hit = [gap == c for c in range(4)]
            where_x = [[edge_x + 4 * m - xbase == c for c in range(4)] for m in range(3)]
            for k in range(3):
                column = []
                for a in range(4):
                    value = none
                    for b in range(3, -1, -1):
                        value = jnp.where(hit[b], tap(16 * k + 4 * b + a), value)
                    column.append(value)
                for m in range(3):
                    value = none
                    for a in range(3, -1, -1):
                        value = jnp.where(where_x[m][a], column[a], value)
                    a_ref[WIN_X * ROWS_Y + TILE * m:WIN_X * ROWS_Y + TILE * (m + 1),
                          (member * 3 + k) * LANES:(member * 3 + k + 1) * LANES] = value
                yield
            bit2 = xbase >= 4
            xbase = xbase - jnp.where(bit2, jnp.full_like(none, 4), none)
            bit1 = xbase >= 2
            xbase = xbase - jnp.where(bit1, jnp.full_like(none, 2), none)
            bit0 = xbase >= 1
            for t in range(ROWS_Y // TILE):
                gap = tile_rows + (TILE * t) - ybase
                hit = [gap == c for c in range(4)]
                for k in range(3):
                    column = []
                    for a in range(4):
                        value = none
                        for b in range(3, -1, -1):
                            value = jnp.where(hit[b], tap(16 * k + 4 * b + a), value)
                        column.append(value)
                    for bit, step in ((bit0, 1), (bit1, 2), (bit2, 4)):
                        size = len(column)
                        column = [
                            jnp.where(bit, column[i - step] if i >= step else none, column[i] if i < size else none)
                            for i in range(size + step)
                        ]
                    for x in range(WIN_X):
                        a_ref[x * ROWS_Y + TILE * t:x * ROWS_Y + TILE * (t + 1),
                              (member * 3 + k) * LANES:(member * 3 + k + 1) * LANES] = column[x]
                    yield

    def push(b_ref, part, unit, register):
        cut = slice(part * 2 * LANES, (part + 1) * 2 * LANES)
        pltpu.matmul_push_rhs(b_ref[:, cut], register, unit, transpose=True)

    def multiply(sums, a_ref, b_ref):
        def add(part, unit, i, register):
            row, size = CHUNKS[i]
            lhs = a_ref[row:row + size, part * 2 * LANES:(part + 1) * 2 * LANES]
            pltpu.matmul_acc_lhs(sums[unit * len(CHUNKS) + i], lhs, load_staged_rhs=register)

        for i in range(len(CHUNKS)):
            for unit in range(2):
                add(unit, unit, i, None if i else 0)
                yield
            if i < 2:
                push(b_ref, 2, i, 1)
        for i in range(len(CHUNKS) // 2):
            for unit in range(2):
                add(2, unit, i + unit * (len(CHUNKS) // 2), None if i else 1)
                yield

    def flush(sums, plane):
        main = WIN_X * ROWS_Y
        first = pl.multiple_of(plane * (XB * ROWS_Y), XB * ROWS_Y)
        corner = pl.multiple_of(plane * (XB * 4), XB * 4)
        for i, (row, size) in enumerate(CHUNKS):
            part = pltpu.matmul_pop(sums[i]) + pltpu.matmul_pop(sums[len(CHUNKS) + i])
            inside = min(size, main - row)
            for half in range(2):
                cut = slice(half * LANES, (half + 1) * LANES)
                grid, rim = density.at[half], edge.at[half]
                grid[pl.ds(first + row, inside), :] = grid[pl.ds(first + row, inside), :] + part[:inside, cut]
                if inside < size:
                    rim[pl.ds(corner, size - inside), :] = rim[pl.ds(corner, size - inside), :] + part[inside:, cut]

    def step(sums, q, now, later, slot):
        steps = multiply(sums, *now)
        for unit in range(2):
            push(now[1], unit, unit, 0)
        for i, _ in enumerate(build(q + 1, *later, slot)):
            if i >= 2 * BUILD_STEPS and i % BUILD_STEPS == 0:
                next(steps, None)
        for _ in steps:
            pass

        @pl.when(pair_last[q] == 1)
        def _():
            flush(sums, pair_plane[q])

    for _ in build(0, a0, b0, 0):
        pass

    def turns(*sums):
        def turn(i, carry):
            step(sums, 2 * i, (a0, b0), (a1, b1), 1)
            step(sums, 2 * i + 1, (a1, b1), (a0, b0), 0)
            return carry

        lax.fori_loop(0, (pairs + 1) // 2, turn, 0)

    pl.run_scoped(turns, *[pltpu.ACC(unit)((size, NZ), F32) for unit in range(2) for _, size in CHUNKS])

    lines = cells_x + 3
    width = rim_ref.shape[0] // lines
    for half in range(2):
        for y in range(3):
            rim_ref[pl.ds(y * 2 + half, lines, stride=width), :] = edge.at[half][pl.ds(y, lines, stride=4), :]
    for r in range(6, width):
        rim_ref[pl.ds(r, lines, stride=width), :] = jnp.zeros((lines, LANES), F32)


def line_kernel(density_ref, out_ref):
    lines = density_ref.shape[1] // ROWS_Y
    width = out_ref.shape[1] // lines
    columns = width // 2
    for half in range(2):
        for y in range(ROWS_Y):
            out_ref[y // columns, pl.ds(y % columns * 2 + half, lines, stride=width), :] = (
                density_ref.at[half][pl.ds(y, lines, stride=ROWS_Y), :]
            )


def x_kernel(groups, cells_x, in_ref, table_ref, out_ref, narrow):
    width = 8
    spilled = lax.broadcasted_iota(jnp.int32, (8, LANES), 0) < 3
    for l in range(width):
        cut = slice(l * LANES, (l + 1) * LANES)
        for src in range(groups):
            own = in_ref[src, pl.ds(l, cells_x, stride=width), :]
            last = in_ref[(src - 1) % groups, pl.ds((cells_x - 5) * width + l, 8, stride=width), :]
            spill = jnp.where(spilled, pltpu.roll(last, 3, axis=0), 0.0)
            narrow[src * cells_x:(src + 1) * cells_x, cut] = jnp.concatenate([own[:8] + spill, own[8:]], 0).astype(BF16)
    half = table_ref.shape[0] // 2
    data = narrow[...]
    result = jnp.dot(table_ref[:half], data, preferred_element_type=F32) + jnp.dot(
        table_ref[half:], data, preferred_element_type=F32
    )
    devices = out_ref.shape[0] // 32
    for q in range(4):
        for l in range(width):
            out_ref[pl.ds(l // 2 * 8 + q * 2 + l % 2, devices, stride=32), :] = (
                result[q * devices:(q + 1) * devices, l * LANES:(l + 1) * LANES]
            )


def y_kernel(in_ref, table_ref, coupling_ref, out_ref, data, spectrum, ready, sent):
    half_y = NY // 2
    sums = []
    for odd in range(2):
        for q in range(4):
            for half in range(2):
                value = in_ref[pl.ds(odd * 8 + q * 2 + half, half_y, stride=16), :]
                same = slice(q * NZ + half * LANES, q * NZ + (half + 1) * LANES)
                swap = slice((q ^ 1) * NZ + half * LANES, (q ^ 1) * NZ + (half + 1) * LANES)
                data[odd, 0:half_y, same] = value.astype(BF16)
                data[odd, half_y:NY, swap] = (value if q % 2 else -value).astype(BF16)
        sums.append(split_dot(table_ref[odd], data[odd]))
    even, odd = sums
    spectrum[0:half_y, :] = (even + odd).astype(BF16)
    spectrum[half_y:NY, :] = (even - odd).astype(BF16)

    block = NY // MBLK
    dims = (((1,), (1,)), ((), ()))
    copies = []
    for b in range(MBLK):
        rows = spectrum[b * block:(b + 1) * block, :]
        rows = jnp.concatenate([rows[:, q * NZ:(q + 1) * NZ] for q in range(4)], axis=0)
        weight = coupling_ref[b]
        high = weight.astype(BF16)
        low = (weight - high.astype(F32)).astype(BF16)
        result = lax.dot_general(rows, high, dims, preferred_element_type=F32) + lax.dot_general(
            rows, low, dims, preferred_element_type=F32
        )
        for q in range(4):
            ready[b, q % 2, q // 2, :, :] = result[q * block:(q + 1) * block]
        copy = pltpu.make_async_copy(ready.at[b], out_ref.at[:, :, pl.ds(b * block, block), :], sent.at[b])
        copy.start()
        copies.append(copy)
    for copy in copies:
        copy.wait()


def two_parts(table):
    high = table.astype(ml_dtypes.bfloat16)
    low = (table - high.astype(np.float64)).astype(ml_dtypes.bfloat16)
    return np.concatenate([high, low], axis=-2)


def split_dot(table, data):
    both = jnp.dot(table, data, preferred_element_type=F32)
    rows = both.shape[0] // 2
    return both[:rows] + both[rows:]


def tables(size_x, size_y):
    devices = size_x * size_y
    wave = np.arange(KX).reshape(devices, 2).T.reshape(2, 1, devices, 1)
    angle = 2.0 * np.pi * (wave * np.arange(NX) % NX) / NX
    scale = 1.0 / math.sqrt(NX * NY)
    table_x = np.concatenate([np.cos(angle), -np.sin(angle)], 1).reshape(4 * devices, NX) * scale
    columns = NY // devices
    y = np.arange(size_y)[None, :, None] * (NY // size_y) + np.arange(size_x)[:, None, None] * columns + np.arange(columns)
    y = y.reshape(NY // 2, 2).T.reshape(2, 1, NY // 2)
    angle = 2.0 * np.pi * (np.arange(NY // 2)[None, :, None] * y % NY) / NY
    table_y = np.concatenate([np.cos(angle), np.sin(angle)], 2)
    return two_parts(table_x), two_parts(table_y)


def make_spread(block_count, cells_x, cells_y, size_x):
    lines = cells_x + 3
    groups = (block_count + 2) * (cells_x // XB) + 2
    vmem = pltpu.VMEM
    slots = block_count * LANES
    whole = pl.BlockSpec(memory_space=pltpu.VMEM)
    return pl.pallas_call(
        lambda *refs: spread_kernel(cells_x, cells_y, block_count, *refs),
        out_shape=(
            jax.ShapeDtypeStruct((2, lines * ROWS_Y, LANES), F32),
            jax.ShapeDtypeStruct((lines * 8, LANES), F32),
        ),
        in_specs=[pl.BlockSpec(memory_space=pltpu.MemorySpace.HBM)] * 5,
        out_specs=(whole, whole),
        scratch_shapes=[
            pltpu.SMEM((block_count,), jnp.int32),
            pltpu.SMEM((block_count,), jnp.int32),
            vmem((10, slots), F32),
            vmem((3, slots), F32),
            vmem((3, slots), jnp.int32),
            pltpu.SemaphoreType.DMA((5,)),
            vmem((groups * TILE, LANES), F32),
            vmem((256, LANES), F32),
            vmem((ROWS, 6 * LANES), BF16),
            vmem((NZ, 6 * LANES), BF16),
            vmem((ROWS, 6 * LANES), BF16),
            vmem((NZ, 6 * LANES), BF16),
            vmem((2, (lines + 1) * 4, LANES), F32),
            vmem((BATCH, TILE, LANES), F32),
            pltpu.SMEM((8,), jnp.int32),
            pltpu.SMEM((block_count + 16,), jnp.int32),
            pltpu.SMEM((block_count + 16,), jnp.int32),
            pltpu.SMEM((block_count + 16,), jnp.int32),
        ],
        compiler_params=pltpu.CompilerParams(vmem_limit_bytes=20 << 20),
        name="spread",
    )


def make_y(size_x, size_y):
    _, table = tables(size_x, size_y)
    vmem = pltpu.VMEM
    call = pl.pallas_call(
        y_kernel,
        out_shape=jax.ShapeDtypeStruct((2, 2, NY, NZ), F32),
        in_specs=[pl.BlockSpec(memory_space=pltpu.VMEM)] * 3,
        out_specs=pl.BlockSpec(memory_space=pltpu.MemorySpace.HBM),
        scratch_shapes=[
            vmem((2, NY, 4 * NZ), BF16),
            vmem((NY, 4 * NZ), BF16),
            vmem((MBLK, 2, 2, NY // MBLK, NZ), F32),
            pltpu.SemaphoreType.DMA((MBLK,)),
        ],
        compiler_params=pltpu.CompilerParams(vmem_limit_bytes=20 << 20),
        name="transform_y",
    )
    return lambda spectrum, coupling: call(spectrum, jnp.asarray(table), coupling)


def per_device(multipoles, fractions, base_index, block_plane, atom_count, coupling):
    size_x = lax.axis_size("gx")
    size_y = lax.axis_size("gy")
    cells_x = NX // size_x
    cells_y = NY // size_y
    block_count = block_plane.shape[0]
    devices = size_x * size_y
    table, _ = tables(size_x, size_y)
    vmem = pltpu.VMEM
    whole = pl.BlockSpec(memory_space=pltpu.VMEM)
    limit = pltpu.CompilerParams(vmem_limit_bytes=20 << 20)

    hbm = pltpu.MemorySpace.HBM
    atoms = (block_plane, atom_count, multipoles, fractions, base_index)
    density, rim = make_spread(block_count, cells_x, cells_y, size_x)(
        *[pltpu.with_memory_space_constraint(array, hbm) for array in atoms]
    )

    rim = lax.ppermute(rim, "gy", [(i, (i + 1) % size_y) for i in range(size_y)])
    density = pl.pallas_call(
        line_kernel,
        out_shape=jax.ShapeDtypeStruct((size_x, (cells_x + 3) * 8, LANES), F32),
        in_specs=[whole],
        out_specs=whole,
        compiler_params=limit,
        name="lines",
    )(density)
    density = density.at[0].add(rim)
    density = lax.all_to_all(density, "gx", split_axis=0, concat_axis=0, tiled=True)

    spectrum = pl.pallas_call(
        lambda *refs: x_kernel(size_x, cells_x, *refs),
        out_shape=jax.ShapeDtypeStruct((devices * 32, LANES), F32),
        in_specs=[whole] * 2,
        out_specs=whole,
        scratch_shapes=[vmem((NX, 8 * LANES), BF16)],
        compiler_params=limit,
        name="transform_x",
    )(density, jnp.asarray(table))

    spectrum = lax.all_to_all(
        spectrum.reshape(devices, 32, LANES), ("gx", "gy"), split_axis=0, concat_axis=0, tiled=True
    ).reshape(devices * 32, LANES)

    return make_y(size_x, size_y)(spectrum, coupling)


def solution(mesh):
    return jax.shard_map(
        per_device,
        mesh=mesh,
        in_specs=(
            P(None, ("gx", "gy")),
            P(None, ("gx", "gy")),
            P(None, ("gx", "gy")),
            P(("gx", "gy")),
            P(("gx", "gy")),
            P(),
        ),
        out_specs=P(None, ("gx", "gy"), None, None),
        check_vma=False,
    )
```

```python
import math

import jax
import jax.numpy as jnp
import ml_dtypes
import numpy as np
from jax import lax
from jax.experimental import pallas as pl
from jax.experimental.pallas import tpu as pltpu
from jax.sharding import PartitionSpec as P

NX = 512
NY = 512
NZ = 256
XB = 8
LANES = 128
MBLK = 8
KX = 256
TILE = 16
ROWS_Y = 64
WIN_X = XB + 3
ROWS = WIN_X * ROWS_Y + 3 * TILE
BATCH = 16
BUILD_STEPS = 3
CHUNKS = ((0, 128), (128, 128), (256, 128), (384, 128), (512, 128), (640, 112))
F32 = jnp.float32
BF16 = jnp.bfloat16


def tap_constants(tap):
    def pick(c0, c1, c2, c3):
        return jnp.where(tap == 0, c0, jnp.where(tap == 1, c1, jnp.where(tap == 2, c2, c3))).astype(F32)

    return dict(
        shift=pick(1.0, 0.0, 0.0, 0.0),
        sign=pick(-1.0, 1.0, 1.0, 1.0),
        w=(pick(0.0, 2.0 / 3.0, 1.0 / 6.0, 0.0), pick(0.0, 0.0, 0.5, 0.0), pick(0.0, -1.0, 0.5, 0.0), pick(1.0 / 6.0, 0.5, -0.5, 1.0 / 6.0)),
        d=(pick(0.0, 0.0, 0.5, 0.0), pick(0.0, -2.0, 1.0, 0.0), pick(-0.5, 1.5, -1.5, 0.5)),
        s=(pick(0.0, -2.0, 1.0, 0.0), pick(1.0, 3.0, -3.0, 1.0)),
    )


def tap_values(fraction, const):
    u = const["shift"] + const["sign"] * fraction
    w0, w1, w2, w3 = const["w"]
    d0, d1, d2 = const["d"]
    s0, s1 = const["s"]
    return ((w3 * u + w2) * u + w1) * u + w0, (d2 * u + d1) * u + d0, s1 * u + s0


def spread_kernel(cells_x, cells_y, block_count, plane_in, count_in, moment_in, fraction_in, base_in, density, rim_ref,
                  plane_ref, count_ref, moment_ref, fraction_ref, base_ref, arrived, raw, taps, a0, b0, a1, b1, edge, stage, cursor, pair_group, pair_plane, pair_last):
    planes = cells_x // XB
    room = block_count + 2
    spare = planes * room
    lane = lax.broadcasted_iota(jnp.int32, (TILE, LANES), 1)

    copies = [
        pltpu.make_async_copy(source, target, arrived.at[i])
        for i, (source, target) in enumerate(
            (
                (plane_in, plane_ref),
                (count_in, count_ref),
                (moment_in, moment_ref),
                (fraction_in, fraction_ref),
                (base_in, base_ref),
            )
        )
    ]
    for copy in copies:
        copy.start()
    density[...] = jnp.zeros_like(density)
    edge[...] = jnp.zeros_like(edge)

    copies[0].wait()
    copies[1].wait()

    zero_group = jnp.zeros((TILE, LANES), F32)
    for p in range(planes):
        cursor[p] = p * room * LANES
        raw[p * room * TILE:(p * room + 1) * TILE, :] = zero_group
    for i in range(2):
        raw[(spare + i) * TILE:(spare + i + 1) * TILE, :] = zero_group

    for copy in copies[2:]:
        copy.wait()

    def append(i, carry):
        moved = []
        for k in range(BATCH):
            g = i * BATCH + k
            column = pl.multiple_of(g * LANES, LANES)
            stage[k, 0:10, :] = moment_ref[:, pl.ds(column, LANES)]
            stage[k, 10:13, :] = fraction_ref[:, pl.ds(column, LANES)]
            stage[k, 13:16, :] = base_ref[:, pl.ds(column, LANES)].astype(F32)
        for k in range(BATCH):
            g = i * BATCH + k
            p = plane_ref[g]
            live = count_ref[g]
            place = cursor[p]
            cursor[p] = place + live
            offset = place % LANES
            rows = pltpu.roll(jnp.where(lane < live, stage[k], 0.0), offset, axis=1)
            moved.append((pl.multiple_of(place // LANES * TILE, TILE), lane >= offset, rows))
        for first, keep, rows in moved:
            raw[pl.ds(first, TILE), :] = raw[pl.ds(first, TILE), :] + jnp.where(keep, rows, 0.0)
            raw[pl.ds(first + TILE, TILE), :] = jnp.where(keep, 0.0, rows)
        return carry

    lax.fori_loop(0, block_count // BATCH, append, 0)
    pairs = jnp.int32(0)
    for p in range(planes):
        start = p * room
        after = (cursor[p] + LANES - 1) // LANES
        raw[pl.ds(pl.multiple_of(after * TILE, TILE), TILE), :] = zero_group
        here = (after - start + 1) // 2

        def note(i, carry, start=start, pairs=pairs, here=here, p=p):
            pair_group[pairs + i] = start + 2 * i
            pair_plane[pairs + i] = p
            pair_last[pairs + i] = jnp.where(i == here - 1, 1, 0)
            return carry

        lax.fori_loop(0, here, note, 0)
        pairs = pairs + here
    for i in range(3):
        pair_group[pairs + i] = spare
        pair_plane[pairs + i] = 0
        pair_last[pairs + i] = 1

    sub = lax.broadcasted_iota(jnp.int32, (8, LANES), 0)
    inner = tap_constants(sub % 4)
    outer = [tap_constants(sub // 4), tap_constants(2 + sub // 4)]
    tile_rows = lax.broadcasted_iota(jnp.int32, (TILE, LANES), 0).astype(F32).astype(BF16)
    none = jnp.zeros((TILE, LANES), BF16)
    tile_iota = lax.broadcasted_iota(jnp.int32, (TILE, LANES), 0)
    edge_x = (tile_iota // 4).astype(F32).astype(BF16)
    edge_y = (cells_y + tile_iota % 4).astype(F32).astype(BF16)

    def build(q, a_ref, b_ref, slot):
        for member in range(2):
            base = (pair_group[q] + member) * TILE
            first = (slot * 2 + member) * 64

            def row(r, base=base):
                return raw[pl.ds(base + r, 8, stride=0), :]

            def wide(r, base=base):
                return raw[pl.ds(base + r, TILE, stride=0), :].astype(BF16)

            def tap(r, first=first):
                return taps[pl.ds(first + r, TILE, stride=0), :].astype(BF16)

            m = [row(r) for r in range(10)]
            wx, dx, sx = tap_values(row(10), inner)
            x0 = m[0] * wx + m[1] * dx + m[4] * sx
            x1 = m[2] * wx + m[7] * dx
            x2 = m[5] * wx
            x3 = m[3] * wx + m[8] * dx
            x4 = m[9] * wx
            x5 = m[6] * wx
            for half in range(2):
                wy, dy, sy = tap_values(row(11), outer[half])
                taps[first + 8 * half:first + 8 * half + 8, :] = x0 * wy + x1 * dy + x2 * sy
                taps[first + 16 + 8 * half:first + 24 + 8 * half, :] = x3 * wy + x4 * dy
                taps[first + 32 + 8 * half:first + 40 + 8 * half, :] = x5 * wy
            wz, dz, sz = tap_values(row(12), inner)
            taps[first + 48:first + 52, :] = wz[0:4]
            taps[first + 52:first + 56, :] = dz[0:4]
            taps[first + 56:first + 60, :] = sz[0:4]

            zbase = wide(15)
            ztap = [[tap(48 + 4 * k + c) for c in range(4)] for k in range(3)]
            for t in range(NZ // TILE):
                gap = tile_rows + (TILE * t) - zbase
                hit = [gap == c for c in range(4)]
                for k in range(3):
                    value = none
                    for c in range(3, -1, -1):
                        value = jnp.where(hit[c], ztap[k][c], value)
                    b_ref[TILE * t:TILE * (t + 1), (member * 3 + k) * LANES:(member * 3 + k + 1) * LANES] = value
                yield

        for member in range(2):
            base = (pair_group[q] + member) * TILE
            first = (slot * 2 + member) * 64

            def wide(r, base=base):
                return raw[pl.ds(base + r, TILE, stride=0), :].astype(BF16)

            def tap(r, first=first):
                return taps[pl.ds(first + r, TILE, stride=0), :].astype(BF16)

            ybase = wide(14)
            xbase = wide(13)
            gap = edge_y - ybase
            hit = [gap == c for c in range(4)]
            where_x = [[edge_x + 4 * m - xbase == c for c in range(4)] for m in range(3)]
            for k in range(3):
                column = []
                for a in range(4):
                    value = none
                    for b in range(3, -1, -1):
                        value = jnp.where(hit[b], tap(16 * k + 4 * b + a), value)
                    column.append(value)
                for m in range(3):
                    value = none
                    for a in range(3, -1, -1):
                        value = jnp.where(where_x[m][a], column[a], value)
                    a_ref[WIN_X * ROWS_Y + TILE * m:WIN_X * ROWS_Y + TILE * (m + 1),
                          (member * 3 + k) * LANES:(member * 3 + k + 1) * LANES] = value
                yield
            bit2 = xbase >= 4
            xbase = xbase - jnp.where(bit2, jnp.full_like(none, 4), none)
            bit1 = xbase >= 2
            xbase = xbase - jnp.where(bit1, jnp.full_like(none, 2), none)
            bit0 = xbase >= 1
            for t in range(ROWS_Y // TILE):
                gap = tile_rows + (TILE * t) - ybase
                hit = [gap == c for c in range(4)]
                for k in range(3):
                    column = []
                    for a in range(4):
                        value = none
                        for b in range(3, -1, -1):
                            value = jnp.where(hit[b], tap(16 * k + 4 * b + a), value)
                        column.append(value)
                    for bit, step in ((bit0, 1), (bit1, 2), (bit2, 4)):
                        size = len(column)
                        column = [
                            jnp.where(bit, column[i - step] if i >= step else none, column[i] if i < size else none)
                            for i in range(size + step)
                        ]
                    for x in range(WIN_X):
                        a_ref[x * ROWS_Y + TILE * t:x * ROWS_Y + TILE * (t + 1),
                              (member * 3 + k) * LANES:(member * 3 + k + 1) * LANES] = column[x]
                    yield

    def push(b_ref, part, unit, register):
        cut = slice(part * 2 * LANES, (part + 1) * 2 * LANES)
        pltpu.matmul_push_rhs(b_ref[:, cut], register, unit, transpose=True)

    def multiply(sums, a_ref, b_ref):
        def add(part, unit, i, register):
            row, size = CHUNKS[i]
            lhs = a_ref[row:row + size, part * 2 * LANES:(part + 1) * 2 * LANES]
            pltpu.matmul_acc_lhs(sums[unit * len(CHUNKS) + i], lhs, load_staged_rhs=register)

        for i in range(len(CHUNKS)):
            for unit in range(2):
                add(unit, unit, i, None if i else 0)
                yield
            if i < 2:
                push(b_ref, 2, i, 1)
        for i in range(len(CHUNKS) // 2):
            for unit in range(2):
                add(2, unit, i + unit * (len(CHUNKS) // 2), None if i else 1)
                yield

    def flush(sums, plane):
        main = WIN_X * ROWS_Y
        first = pl.multiple_of(plane * (XB * ROWS_Y), XB * ROWS_Y)
        corner = pl.multiple_of(plane * (XB * 4), XB * 4)
        for i, (row, size) in enumerate(CHUNKS):
            part = pltpu.matmul_pop(sums[i]) + pltpu.matmul_pop(sums[len(CHUNKS) + i])
            inside = min(size, main - row)
            for half in range(2):
                cut = slice(half * LANES, (half + 1) * LANES)
                grid, rim = density.at[half], edge.at[half]
                grid[pl.ds(first + row, inside), :] = grid[pl.ds(first + row, inside), :] + part[:inside, cut]
                if inside < size:
                    rim[pl.ds(corner, size - inside), :] = rim[pl.ds(corner, size - inside), :] + part[inside:, cut]

    def step(sums, q, now, later, slot):
        steps = multiply(sums, *now)
        for unit in range(2):
            push(now[1], unit, unit, 0)
        for i, _ in enumerate(build(q + 1, *later, slot)):
            if i >= 2 * BUILD_STEPS and i % BUILD_STEPS == 0:
                next(steps, None)
        for _ in steps:
            pass

        @pl.when(pair_last[q] == 1)
        def _():
            flush(sums, pair_plane[q])

    for _ in build(0, a0, b0, 0):
        pass

    def turns(*sums):
        def turn(i, carry):
            step(sums, 2 * i, (a0, b0), (a1, b1), 1)
            step(sums, 2 * i + 1, (a1, b1), (a0, b0), 0)
            return carry

        lax.fori_loop(0, (pairs + 1) // 2, turn, 0)

    pl.run_scoped(turns, *[pltpu.ACC(unit)((size, NZ), F32) for unit in range(2) for _, size in CHUNKS])

    lines = cells_x + 3
    width = rim_ref.shape[0] // lines
    for half in range(2):
        for y in range(3):
            rim_ref[pl.ds(y * 2 + half, lines, stride=width), :] = edge.at[half][pl.ds(y, lines, stride=4), :]
    for r in range(6, width):
        rim_ref[pl.ds(r, lines, stride=width), :] = jnp.zeros((lines, LANES), F32)


def line_kernel(density_ref, out_ref):
    lines = density_ref.shape[1] // ROWS_Y
    width = out_ref.shape[1] // lines
    columns = width // 2
    for half in range(2):
        for y in range(ROWS_Y):
            out_ref[y // columns, pl.ds(y % columns * 2 + half, lines, stride=width), :] = (
                density_ref.at[half][pl.ds(y, lines, stride=ROWS_Y), :]
            )


def x_kernel(groups, cells_x, in_ref, table_ref, out_ref, narrow):
    width = 8
    spilled = lax.broadcasted_iota(jnp.int32, (8, LANES), 0) < 3
    for l in range(width):
        cut = slice(l * LANES, (l + 1) * LANES)
        for src in range(groups):
            own = in_ref[src, pl.ds(l, cells_x, stride=width), :]
            last = in_ref[(src - 1) % groups, pl.ds((cells_x - 5) * width + l, 8, stride=width), :]
            spill = jnp.where(spilled, pltpu.roll(last, 3, axis=0), 0.0)
            narrow[src * cells_x:(src + 1) * cells_x, cut] = jnp.concatenate([own[:8] + spill, own[8:]], 0).astype(BF16)
    half = table_ref.shape[0] // 2
    data = narrow[...]
    result = jnp.dot(table_ref[:half], data, preferred_element_type=F32) + jnp.dot(
        table_ref[half:], data, preferred_element_type=F32
    )
    devices = out_ref.shape[0] // 32
    for q in range(4):
        for l in range(width):
            out_ref[pl.ds(l // 2 * 8 + q * 2 + l % 2, devices, stride=32), :] = (
                result[q * devices:(q + 1) * devices, l * LANES:(l + 1) * LANES]
            )


def y_kernel(in_ref, table_ref, coupling_ref, out_ref, data, spectrum, ready, sent):
    half_y = NY // 2
    sums = []
    for odd in range(2):
        for q in range(4):
            for half in range(2):
                value = in_ref[pl.ds(odd * 8 + q * 2 + half, half_y, stride=16), :]
                same = slice(q * NZ + half * LANES, q * NZ + (half + 1) * LANES)
                swap = slice((q ^ 1) * NZ + half * LANES, (q ^ 1) * NZ + (half + 1) * LANES)
                data[odd, 0:half_y, same] = value.astype(BF16)
                data[odd, half_y:NY, swap] = (value if q % 2 else -value).astype(BF16)
        sums.append(split_dot(table_ref[odd], data[odd]))
    even, odd = sums
    spectrum[0:half_y, :] = (even + odd).astype(BF16)
    spectrum[half_y:NY, :] = (even - odd).astype(BF16)

    block = NY // MBLK
    dims = (((1,), (1,)), ((), ()))
    copies = []
    for b in range(MBLK):
        rows = spectrum[b * block:(b + 1) * block, :]
        rows = jnp.concatenate([rows[:, q * NZ:(q + 1) * NZ] for q in range(4)], axis=0)
        weight = coupling_ref[b]
        high = weight.astype(BF16)
        low = (weight - high.astype(F32)).astype(BF16)
        result = lax.dot_general(rows, high, dims, preferred_element_type=F32) + lax.dot_general(
            rows, low, dims, preferred_element_type=F32
        )
        for q in range(4):
            ready[b, q % 2, q // 2, :, :] = result[q * block:(q + 1) * block]
        copy = pltpu.make_async_copy(ready.at[b], out_ref.at[:, :, pl.ds(b * block, block), :], sent.at[b])
        copy.start()
        copies.append(copy)
    for copy in copies:
        copy.wait()


def two_parts(table):
    high = table.astype(ml_dtypes.bfloat16)
    low = (table - high.astype(np.float64)).astype(ml_dtypes.bfloat16)
    return np.concatenate([high, low], axis=-2)


def split_dot(table, data):
    both = jnp.dot(table, data, preferred_element_type=F32)
    rows = both.shape[0] // 2
    return both[:rows] + both[rows:]


def tables(size_x, size_y):
    devices = size_x * size_y
    wave = np.arange(KX).reshape(devices, 2).T.reshape(2, 1, devices, 1)
    angle = 2.0 * np.pi * (wave * np.arange(NX) % NX) / NX
    scale = 1.0 / math.sqrt(NX * NY)
    table_x = np.concatenate([np.cos(angle), -np.sin(angle)], 1).reshape(4 * devices, NX) * scale
    columns = NY // devices
    y = np.arange(size_y)[None, :, None] * (NY // size_y) + np.arange(size_x)[:, None, None] * columns + np.arange(columns)
    y = y.reshape(NY // 2, 2).T.reshape(2, 1, NY // 2)
    angle = 2.0 * np.pi * (np.arange(NY // 2)[None, :, None] * y % NY) / NY
    table_y = np.concatenate([np.cos(angle), np.sin(angle)], 2)
    return two_parts(table_x), two_parts(table_y)


def make_spread(block_count, cells_x, cells_y, size_x):
    lines = cells_x + 3
    groups = (block_count + 2) * (cells_x // XB) + 2
    vmem = pltpu.VMEM
    slots = block_count * LANES
    whole = pl.BlockSpec(memory_space=pltpu.VMEM)
    return pl.pallas_call(
        lambda *refs: spread_kernel(cells_x, cells_y, block_count, *refs),
        out_shape=(
            jax.ShapeDtypeStruct((2, lines * ROWS_Y, LANES), F32),
            jax.ShapeDtypeStruct((lines * 8, LANES), F32),
        ),
        in_specs=[pl.BlockSpec(memory_space=pltpu.MemorySpace.HBM)] * 5,
        out_specs=(whole, whole),
        scratch_shapes=[
            pltpu.SMEM((block_count,), jnp.int32),
            pltpu.SMEM((block_count,), jnp.int32),
            vmem((10, slots), F32),
            vmem((3, slots), F32),
            vmem((3, slots), jnp.int32),
            pltpu.SemaphoreType.DMA((5,)),
            vmem((groups * TILE, LANES), F32),
            vmem((256, LANES), F32),
            vmem((ROWS, 6 * LANES), BF16),
            vmem((NZ, 6 * LANES), BF16),
            vmem((ROWS, 6 * LANES), BF16),
            vmem((NZ, 6 * LANES), BF16),
            vmem((2, (lines + 1) * 4, LANES), F32),
            vmem((BATCH, TILE, LANES), F32),
            pltpu.SMEM((8,), jnp.int32),
            pltpu.SMEM((block_count + 16,), jnp.int32),
            pltpu.SMEM((block_count + 16,), jnp.int32),
            pltpu.SMEM((block_count + 16,), jnp.int32),
        ],
        compiler_params=pltpu.CompilerParams(vmem_limit_bytes=20 << 20),
        name="spread",
    )


def make_y(size_x, size_y):
    _, table = tables(size_x, size_y)
    vmem = pltpu.VMEM
    call = pl.pallas_call(
        y_kernel,
        out_shape=jax.ShapeDtypeStruct((2, 2, NY, NZ), F32),
        in_specs=[pl.BlockSpec(memory_space=pltpu.VMEM)] * 3,
        out_specs=pl.BlockSpec(memory_space=pltpu.MemorySpace.HBM),
        scratch_shapes=[
            vmem((2, NY, 4 * NZ), BF16),
            vmem((NY, 4 * NZ), BF16),
            vmem((MBLK, 2, 2, NY // MBLK, NZ), F32),
            pltpu.SemaphoreType.DMA((MBLK,)),
        ],
        compiler_params=pltpu.CompilerParams(vmem_limit_bytes=20 << 20),
        name="transform_y",
    )
    return lambda spectrum, coupling: call(spectrum, jnp.asarray(table), coupling)


def per_device(multipoles, fractions, base_index, block_plane, atom_count, coupling):
    size_x = lax.axis_size("gx")
    size_y = lax.axis_size("gy")
    cells_x = NX // size_x
    cells_y = NY // size_y
    block_count = block_plane.shape[0]
    devices = size_x * size_y
    table, _ = tables(size_x, size_y)
    vmem = pltpu.VMEM
    whole = pl.BlockSpec(memory_space=pltpu.VMEM)
    limit = pltpu.CompilerParams(vmem_limit_bytes=20 << 20)

    hbm = pltpu.MemorySpace.HBM
    atoms = (block_plane, atom_count, multipoles, fractions, base_index)
    density, rim = make_spread(block_count, cells_x, cells_y, size_x)(
        *[pltpu.with_memory_space_constraint(array, hbm) for array in atoms]
    )

    rim = lax.ppermute(rim, "gy", [(i, (i + 1) % size_y) for i in range(size_y)])
    density = pl.pallas_call(
        line_kernel,
        out_shape=jax.ShapeDtypeStruct((size_x, (cells_x + 3) * 8, LANES), F32),
        in_specs=[whole],
        out_specs=whole,
        compiler_params=limit,
        name="lines",
    )(density)
    density = density.at[0].add(rim)
    density = lax.all_to_all(density, "gx", split_axis=0, concat_axis=0, tiled=True)

    spectrum = pl.pallas_call(
        lambda *refs: x_kernel(size_x, cells_x, *refs),
        out_shape=jax.ShapeDtypeStruct((devices * 32, LANES), F32),
        in_specs=[whole] * 2,
        out_specs=whole,
        scratch_shapes=[vmem((NX, 8 * LANES), BF16)],
        compiler_params=limit,
        name="transform_x",
    )(density, jnp.asarray(table))

    spectrum = lax.all_to_all(
        spectrum.reshape(devices, 32, LANES), ("gx", "gy"), split_axis=0, concat_axis=0, tiled=True
    ).reshape(devices * 32, LANES)

    return make_y(size_x, size_y)(spectrum, coupling)


def solution(mesh):
    return jax.shard_map(
        per_device,
        mesh=mesh,
        in_specs=(
            P(None, ("gx", "gy")),
            P(None, ("gx", "gy")),
            P(None, ("gx", "gy")),
            P(("gx", "gy")),
            P(("gx", "gy")),
            P(),
        ),
        out_specs=P(None, ("gx", "gy"), None, None),
        check_vma=False,
    )
```
